32 devices in a mesh: dp: 8 (over y, x, core), head: 4 (over z).
Axes of the slice: x: 2, y: 2, z: 4, core: 2. Of those that a mesh axis runs over, the one named last changes fastest.
Arguments:
- tokens: bfloat16 [8192, 2048], P('dp'), may hold values from -6 to 6
- cotangent: bfloat16 [8192, 2048], P('dp'), may hold values from -6 to 6
- lengths: int32 [8], P('dp'), may hold values from 256 to 1024, as said below
- attention_gain: float32 [2048], replicated, may hold values from 0.5 to 1.5
- feedforward_gain: float32 [2048], replicated, may hold values from 0.5 to 1.5
- attention_base: bfloat16 [3, 2048, 2048], P(None, 'dp', 'head'), may hold values from -0.125 to 0.125
- output_base: bfloat16 [2048, 2048], P('head', 'dp'), may hold values from -0.125 to 0.125
- gating_base: bfloat16 [2, 2048, 5632], P(None, 'dp', 'head'), may hold values from -0.125 to 0.125
- downward_base: bfloat16 [5632, 2048], P('head', 'dp'), may hold values from -0.078125 to 0.078125
- attention_inner: float32 [3, 2048, 16], replicated, may hold values from -0.125 to 0.125
- attention_outer: float32 [3, 16, 2048], P(None, None, 'head'), may hold values from -0.3 to 0.3
- attention_magnitude: float32 [3, 2048], P(None, 'head'), may hold values from 0.7 to 1.6
- output_inner: float32 [2048, 16], P('head'), may hold values from -0.125 to 0.125
- output_outer_factor: float32 [16, 2048], replicated, may hold values from -0.3 to 0.3
- output_magnitude: float32 [2048], replicated, may hold values from 2 to 8
- gating_inner: float32 [2, 2048, 16], replicated, may hold values from -0.125 to 0.125
- gating_outer: float32 [2, 16, 5632], P(None, None, 'head'), may hold values from -0.3 to 0.3
- gating_magnitude: float32 [2, 5632], P(None, 'head'), may hold values from 0.7 to 2
- downward_inner: float32 [5632, 16], P('head'), may hold values from -0.078125 to 0.078125
- down_outer_factor: float32 [16, 2048], replicated, may hold values from -0.3 to 0.3
- downward_magnitude: float32 [2048], replicated, may hold values from 1 to 4
Outputs:
- output: bfloat16 [8192, 2048], P('dp')
- grad_tokens: float32 [8192, 2048], P('dp')
- attention_ingrad: float32 [3, 2048, 16], replicated
- attention_outgrad: float32 [3, 16, 2048], P(None, None, 'head')
- attention_maggrad: float32 [3, 2048], P(None, 'head')
- output_ingrad: float32 [2048, 16], P('head')
- output_outgrad: float32 [16, 2048], replicated
- output_maggrad: float32 [2048], replicated
- gating_ingrad: float32 [2, 2048, 16], replicated
- gating_outgrad: float32 [2, 16, 5632], P(None, None, 'head')
- gating_maggrad: float32 [2, 5632], P(None, 'head')
- downward_ingrad: float32 [5632, 16], P('head')
- downward_outgrad: float32 [16, 2048], replicated
- downward_maggrad: float32 [2048], replicated
The draws below stay inside these ranges and needn't reach their ends.
Inputs may be any that keep to these rules, and one draw needn't show every extreme that they name: `lengths`: the number of valid leading positions of each row; the rest of the row is padding.
All inputs are finite; a program needn't handle non-finite values.
Results may differ from the reference program's by a relative error of at most 0.028.
Values may be sent and summed in bfloat16 or wider, within the bound.
No kernel may reach another device: no remote copies, remote signals or barrier semaphores. Data moves between devices by JAX's collectives and lax.ppermute only.
A program may use at most 256 MiB of HBM per device.

```python
import math
import jax
import jax.numpy as jnp
from jax import lax

D = 2048
HEADS = 16
HEAD_DIM = 128
FF = 5632
ADAPTER_RANK = 16
ADAPTER_ALPHA = 32
LEN = 1024
SEQS = 8
TOKENS = 8192


def draw_lengths(key, part):
    values = jax.random.randint(jax.random.fold_in(key, 11), (SEQS,), LEN // 4, LEN + 1)
    longest = jax.random.randint(jax.random.fold_in(key, 12), (), 0, SEQS)
    stride = jax.random.randint(jax.random.fold_in(key, 13), (), 1, SEQS)
    shortest = (longest + stride) % SEQS
    position = jnp.arange(SEQS)
    values = jnp.where(position == longest, LEN, values)
    values = jnp.where(position == shortest, LEN // 4, values)
    return values.astype(jnp.int32)


def level_of(rng, dims, pieces, smallest, top_value):
    loudness = 1.0
    for dim, shards_of in pieces:
        heights = jax.random.uniform(jax.random.fold_in(jax.random.fold_in(rng, 6), dim), (shards_of,), jnp.float32, smallest / len(pieces), top_value / len(pieces))
        loudness = loudness * jnp.repeat(jnp.exp(heights), dims[dim] // shards_of).reshape((-1,) + (1,) * (len(dims) - 1 - dim))
    return loudness


def gaussian(stream_key, shape, deviation, limit, pieces=(), dtype=jnp.bfloat16):
    gain = level_of(stream_key, shape, pieces, -0.22, 0.18) if pieces else 1.0
    values = jax.random.normal(stream_key, shape, jnp.float32) * deviation * gain
    return jnp.minimum(jnp.maximum(values, -limit), limit).astype(dtype)


def setup_inputs(seed: int = 0) -> dict:
    keys = jax.random.split(jax.random.key(seed), 22)
    tokens = gaussian(keys[0], (TOKENS, D), 1.0, 6.0, ((0, 8),))
    cotangent = gaussian(keys[1], (TOKENS, D), 1.0, 6.0, ((0, 8),))
    lengths = draw_lengths(jax.random.fold_in(keys[21], 71), 0)
    attention_gain = jnp.clip(1.0 + 0.1 * jax.random.normal(keys[3], (D,), jnp.float32), 0.5, 1.5)
    feedforward_gain = jnp.clip(1.0 + 0.1 * jax.random.normal(keys[4], (D,), jnp.float32), 0.5, 1.5)
    attention_base = gaussian(keys[5], (3, D, D), D ** -0.5, 0.125, ((1, 8), (2, 4)))
    output_base = gaussian(keys[6], (D, D), D ** -0.5, 0.125, ((0, 4), (1, 8)))
    gating_base = gaussian(keys[7], (2, D, FF), D ** -0.5, 0.125, ((1, 8), (2, 4)))
    downward_base = gaussian(keys[8], (FF, D), FF ** -0.5, 0.078125, ((0, 4), (1, 8)))
    attention_inner = gaussian(keys[9], (3, D, ADAPTER_RANK), D ** -0.5, 0.125, (), jnp.float32)
    attention_outer = gaussian(keys[10], (3, ADAPTER_RANK, D), 0.05, 0.3, ((2, 4),), jnp.float32)
    attention_magnitude = jnp.clip(jnp.exp(math.log(1.6) - 0.82667861 * jax.random.uniform(keys[11], (3, D), jnp.float32) ** level_of(keys[11], (3, D), ((1, 4),), -0.2, 0.2)), 0.7, 1.6)
    output_inner = gaussian(keys[12], (D, ADAPTER_RANK), D ** -0.5, 0.125, ((0, 4),), jnp.float32)
    output_outer_factor = gaussian(keys[13], (ADAPTER_RANK, D), 0.05, 0.3, (), jnp.float32)
    output_magnitude = jnp.clip(jnp.exp(jax.random.uniform(keys[14], (D,), jnp.float32, math.log(2.0), math.log(8.0))), 2.0, 8.0)
    gating_inner = gaussian(keys[15], (2, D, ADAPTER_RANK), D ** -0.5, 0.125, (), jnp.float32)
    gating_outer = gaussian(keys[16], (2, ADAPTER_RANK, FF), 0.05, 0.3, ((2, 4),), jnp.float32)
    gating_magnitude = jnp.clip(jnp.exp(math.log(2.0) - 1.0498221 * jax.random.uniform(keys[17], (2, FF), jnp.float32) ** level_of(keys[17], (2, FF), ((1, 4),), -0.2, 0.2)), 0.7, 2.0)
    downward_inner = gaussian(keys[18], (FF, ADAPTER_RANK), FF ** -0.5, 0.078125, ((0, 4),), jnp.float32)
    down_outer_factor = gaussian(keys[19], (ADAPTER_RANK, D), 0.05, 0.3, (), jnp.float32)
    downward_magnitude = jnp.clip(jnp.exp(jax.random.uniform(keys[20], (D,), jnp.float32, math.log(1.0), math.log(4.0))), 1.0, 4.0)
    return {"tokens": tokens, "cotangent": cotangent, "lengths": lengths, "attention_gain": attention_gain, "feedforward_gain": feedforward_gain, "attention_base": attention_base, "output_base": output_base, "gating_base": gating_base, "downward_base": downward_base, "attention_inner": attention_inner, "attention_outer": attention_outer, "attention_magnitude": attention_magnitude, "output_inner": output_inner, "output_outer_factor": output_outer_factor, "output_magnitude": output_magnitude, "gating_inner": gating_inner, "gating_outer": gating_outer, "gating_magnitude": gating_magnitude, "downward_inner": downward_inner, "down_outer_factor": down_outer_factor, "downward_magnitude": downward_magnitude}


@jax.custom_vjp
def low(v):
    return lax.optimization_barrier(v.astype(jnp.bfloat16)).astype(jnp.float32)

@jax.custom_vjp
def reduced_backward(v):
    return v

def low_keep(v):
    return (low(v), None)

def low_pass(kept, grad):
    return (grad,)

def back_keep(v):
    return (v, None)

def back_low(kept, grad):
    return (low(grad),)
low.defvjp(low_keep, low_pass)
reduced_backward.defvjp(back_keep, back_low)
EPS = 1e-05
NORM_EPS = 1e-06
PRECISION_LEVEL = lax.Precision.HIGHEST
NEG = -1e+30

def precise_product(left_mat, right_mat):
    return jnp.dot(left_mat, right_mat, precision=PRECISION_LEVEL, preferred_element_type=jnp.float32)

def rms_norm(values, gain_vec):
    return values * lax.rsqrt(lax.optimization_barrier(jnp.mean(values * values, axis=-1, keepdims=True)) + EPS) * gain_vec

def rotary_tables(total_rows, head_width):
    position = jnp.arange(total_rows).astype(jnp.float32)[:, None]
    inverse = 10000.0 ** (-jnp.arange(0, head_width, 2).astype(jnp.float32) / head_width)
    angles = position * inverse[None, :]
    angles = jnp.concatenate([angles, angles], axis=1)
    return (jnp.cos(angles), jnp.sin(angles))

def rotate(values, cosine_table, sine_table):
    half_width = values.shape[-1] // 2
    turned = jnp.concatenate([-values[..., half_width:], values[..., :half_width]], axis=-1)
    return values * cosine_table[:, None, :] + turned * sine_table[:, None, :]

def dora(input_rows, base_matrix, inner_matrix, outer_matrix, magnitude):
    adapter_scale = ADAPTER_ALPHA / ADAPTER_RANK
    combined_weight = base_matrix + adapter_scale * precise_product(inner_matrix, outer_matrix)
    column_norm = jnp.sqrt(lax.optimization_barrier(jnp.sum(combined_weight * combined_weight, axis=0)) + NORM_EPS)
    summed_total = reduced_backward(precise_product(input_rows, base_matrix) + adapter_scale * precise_product(precise_product(input_rows, inner_matrix), outer_matrix))
    return summed_total * (magnitude / column_norm)

def swiglu(gate_out, up_out):
    return gate_out / (1.0 + jnp.exp(-gate_out)) * up_out

def attend(queries, key_vecs, value_vecs, length):
    total_rows = queries.shape[0]
    scores = jnp.einsum('qhd,khd->hqk', queries, key_vecs, precision=PRECISION_LEVEL) * HEAD_DIM ** (-0.5)
    scores = reduced_backward(scores)
    position = jnp.arange(total_rows)
    allowed = (position[None, :] <= position[:, None]) & (position[None, :] < length)
    scores = jnp.where(allowed[None], scores, NEG)
    shifted = jnp.exp(scores - lax.optimization_barrier(jnp.max(scores, axis=-1, keepdims=True)))
    weights = low(shifted / lax.optimization_barrier(jnp.sum(shifted, axis=-1, keepdims=True)))
    return jnp.einsum('hqk,khd->qhd', weights, value_vecs, precision=PRECISION_LEVEL)

def layer(residual, length, first_gain, second_gain, bases, adapters):
    attention_base, output_base, gating_base, downward_base = bases
    attention_inner = adapters[0]
    attention_outer = adapters[1]
    attention_magnitude = adapters[2]
    output_inner = adapters[3]
    output_outer_factor = adapters[4]
    output_magnitude = adapters[5]
    gating_inner = adapters[6]
    gating_outer = adapters[7]
    gating_magnitude = adapters[8]
    downward_inner = adapters[9]
    down_outer_factor = adapters[10]
    downward_magnitude = adapters[11]
    total_rows = residual.shape[0]
    normed = low(rms_norm(residual, first_gain))
    projected = [dora(normed, attention_base[member], attention_inner[member], attention_outer[member], attention_magnitude[member]) for member in range(3)]
    cosine_table, sine_table = rotary_tables(total_rows, HEAD_DIM)
    queries = low(rotate(projected[0].reshape(total_rows, HEADS, HEAD_DIM), cosine_table, sine_table))
    key_vecs = low(rotate(projected[1].reshape(total_rows, HEADS, HEAD_DIM), cosine_table, sine_table))
    value_vecs = low(projected[2].reshape(total_rows, HEADS, HEAD_DIM))
    attended = attend(queries, key_vecs, value_vecs, length).reshape(total_rows, D)
    attended = low(reduced_backward(attended))
    middle = residual + dora(attended, output_base, output_inner, output_outer_factor, output_magnitude)
    second = low(rms_norm(middle, second_gain))
    gate_out = dora(second, gating_base[0], gating_inner[0], gating_outer[0], gating_magnitude[0])
    up_out = dora(second, gating_base[1], gating_inner[1], gating_outer[1], gating_magnitude[1])
    hidden = low(reduced_backward(swiglu(gate_out, up_out)))
    valid_rows = (jnp.arange(total_rows) < length)[:, None]
    return jnp.where(valid_rows, middle + dora(hidden, downward_base, downward_inner, down_outer_factor, downward_magnitude), 0.0)

def reference(tokens, cotangent, lengths, attention_gain, feedforward_gain, attention_base, output_base, gating_base, downward_base, attention_inner, attention_outer, attention_magnitude, output_inner, output_outer_factor, output_magnitude, gating_inner, gating_outer, gating_magnitude, downward_inner, down_outer_factor, downward_magnitude):
    bases = tuple((element.astype(jnp.float32) for element in (attention_base, output_base, gating_base, downward_base)))
    adapters = tuple((element.astype(jnp.float32) for element in (attention_inner, attention_outer, attention_magnitude, output_inner, output_outer_factor, output_magnitude, gating_inner, gating_outer, gating_magnitude, downward_inner, down_outer_factor, downward_magnitude)))
    first_gain = attention_gain.astype(jnp.float32)
    second_gain = feedforward_gain.astype(jnp.float32)
    rows_all = tokens.astype(jnp.float32).reshape(SEQS, LEN, D)
    seeds_all = cotangent.astype(jnp.float32).reshape(SEQS, LEN, D)

    def one_row(running, element):
        inputs_row, seed_row, length = element

        def forward(residual, *params):
            return layer(residual, length, first_gain, second_gain, bases, params)
        output_row, pull_back = jax.vjp(forward, inputs_row, *adapters)
        gradients = pull_back(seed_row)
        running = tuple((earlier + addend for earlier, addend in zip(running, gradients[1:])))
        return (running, (output_row.astype(jnp.bfloat16), gradients[0]))
    start_sums = tuple((jnp.zeros_like(element) for element in adapters))
    running, (outputs, input_grads) = lax.scan(one_row, start_sums, (rows_all, seeds_all, lengths))
    return (outputs.reshape(TOKENS, D), input_grads.reshape(TOKENS, D), running[0], running[1], running[2], running[3], running[4], running[5], running[6], running[7], running[8], running[9], running[10], running[11])
```

```python
import jax
import jax.numpy as jnp
from jax import lax
from jax.sharding import PartitionSpec as P

HEAD_DIM = 128
SCALE = 2.0
EPS = 1e-05
NORM_EPS = 1e-06
NEG = -1e30
BF = jnp.bfloat16
F32 = jnp.float32


def mm(spec, a, b):
    return jnp.einsum(spec, a.astype(BF), b.astype(BF), preferred_element_type=F32)


def rotary_tables(total_rows):
    position = jnp.arange(total_rows).astype(F32)[:, None]
    inverse = 10000.0 ** (-jnp.arange(0, HEAD_DIM, 2).astype(F32) / HEAD_DIM)
    angles = position * inverse[None, :]
    angles = jnp.concatenate([angles, angles], axis=1)
    return jnp.cos(angles), jnp.sin(angles)


def rotate(values, cosine, sine):
    half = HEAD_DIM // 2
    turned = jnp.concatenate([-values[..., half:], values[..., :half]], axis=-1)
    return values * cosine[:, None, :] + turned * sine[:, None, :]


def rotate_back(grads, cosine, sine):
    half = HEAD_DIM // 2
    scaled = grads * sine[:, None, :]
    turned = jnp.concatenate([scaled[..., half:], -scaled[..., :half]], axis=-1)
    return grads * cosine[:, None, :] + turned


def norm_scale(values):
    return lax.rsqrt(jnp.mean(values * values, axis=-1, keepdims=True) + EPS)


def norm_back(values, gain, grad):
    r = norm_scale(values)
    a = gain * grad
    return r * a - values * (r * r * r) * jnp.mean(values * a, axis=-1, keepdims=True)


class Line:
    def __init__(self, size):
        self.size = size
        self.mid = None
        self.out = None
        self.queue = []
        self.results = {}

    def step(self, name=None, chunk=None):
        if self.size != 4:
            if chunk is not None:
                self.results[name] = lax.psum(chunk, "head")
            return
        new = None if chunk is None else (name, chunk)
        live = [v for v in (new, self.mid, self.out) if v is not None]
        if not live:
            return
        held = lax.optimization_barrier(tuple(v[1] for v in live))
        held = dict(zip([v[0] for v in live], held))
        index = lax.axis_index("head")
        end = (index == 0) | (index == 3)
        nxt_mid = nxt_out = None
        sent = {}
        if new is not None:
            sent["in"] = lax.ppermute(held[new[0]], "head", [(0, 1), (3, 2)])
        if self.mid is not None:
            sent["mid"] = lax.ppermute(held[self.mid[0]], "head", [(1, 2), (2, 1)])
        if self.out is not None:
            sent["out"] = lax.ppermute(held[self.out[0]], "head", [(1, 0), (2, 3)])
        keys = list(sent)
        sent = dict(zip(keys, lax.optimization_barrier(tuple(sent[k] for k in keys))))
        if self.out is not None:
            self.results[self.out[0]] = jnp.where(end, sent["out"], held[self.out[0]])
        if self.mid is not None:
            nxt_out = (self.mid[0], held[self.mid[0]] + sent["mid"])
        if new is not None:
            nxt_mid = (new[0], held[new[0]] + sent["in"])
        self.mid, self.out = nxt_mid, nxt_out


def attend_chunk(q, k, v, length, offset, rows):
    keys = offset + rows
    scores = mm("qhd,khd->hqk", q[offset : offset + rows], k[:keys]) * HEAD_DIM ** (-0.5)
    ki = jnp.arange(keys)
    qi = jnp.arange(offset, offset + rows)
    allowed = (ki[None, :] <= qi[:, None]) & (ki[None, :] < length)
    scores = jnp.where(allowed[None], scores, NEG)
    top = jnp.max(scores, axis=-1, keepdims=True)
    shifted = jnp.exp(scores - top)
    total = jnp.sum(shifted, axis=-1, keepdims=True)
    weights = (shifted / total).astype(BF)
    return mm("hqk,khd->qhd", weights, v[:keys]), top + jnp.log(total)


def attend_back_chunk(q, k, v, grad, logs, length, offset, rows):
    keys = offset + rows
    factor = HEAD_DIM ** (-0.5)
    qc = q[offset : offset + rows]
    scores = mm("qhd,khd->hqk", qc, k[:keys]) * factor
    ki = jnp.arange(keys)
    qi = jnp.arange(offset, offset + rows)
    allowed = (ki[None, :] <= qi[:, None]) & (ki[None, :] < length)
    weights = jnp.exp(jnp.where(allowed[None], scores, NEG) - logs)
    dv = mm("hqk,qhd->khd", weights, grad)
    dw = mm("qhd,khd->hqk", grad, v[:keys])
    ds = (weights * (dw - jnp.sum(weights * dw, axis=-1, keepdims=True))).astype(BF)
    dq = mm("hqk,khd->qhd", ds, k[:keys]) * factor
    dk = mm("hqk,qhd->khd", ds, qc) * factor
    return dq, dk, dv


def make(mesh):
    head_size = mesh.shape["head"]
    dp_size = mesh.shape["dp"]

    def on_device(
        tokens,
        cotangent,
        lengths,
        attention_gain,
        feedforward_gain,
        attention_base,
        output_base,
        gating_base,
        downward_base,
        attention_inner,
        attention_outer,
        attention_magnitude,
        output_inner,
        output_outer_factor,
        output_magnitude,
        gating_inner,
        gating_outer,
        gating_magnitude,
        downward_inner,
        down_outer_factor,
        downward_magnitude,
    ):
        rows, width = tokens.shape
        length = lengths[0]
        dp = lax.axis_index("dp")
        in_rows = attention_base.shape[1]
        out_cols = output_base.shape[1]
        attn_cols = attention_base.shape[2]
        gate_cols = gating_base.shape[2]
        heads = attn_cols // HEAD_DIM
        step_rows = min(256, rows)
        chunks = rows // step_rows

        def merge_column(base, inner, outer):
            part = lax.dynamic_slice_in_dim(inner, dp * in_rows, in_rows, axis=1)
            low = mm("prk,pkc->prc", part, outer)
            return base.astype(F32) + SCALE * low

        def merge_row(base, inner, outer):
            part = lax.dynamic_slice_in_dim(outer, dp * out_cols, out_cols, axis=1)
            return base.astype(F32) + SCALE * mm("rk,kc->rc", inner, part)

        attn_part = merge_column(attention_base, attention_inner, attention_outer).astype(BF)
        attn_w = lax.all_gather(attn_part, "dp", axis=1, tiled=True)
        out_wide = merge_row(output_base, output_inner, output_outer_factor)
        down_wide = merge_row(downward_base, downward_inner, down_outer_factor)
        gate_part = merge_column(gating_base, gating_inner, gating_outer).astype(BF)
        row_squares = jnp.stack(
            [jnp.sum(out_wide * out_wide, axis=0), jnp.sum(down_wide * down_wide, axis=0)]
        )
        attn_w, row_squares, out_part, gate_part = lax.optimization_barrier(
            (attn_w, row_squares, out_wide.astype(BF), gate_part)
        )
        row_squares = lax.all_gather(row_squares, ("dp", "head"), axis=0, tiled=False)
        row_squares = row_squares.reshape(dp_size, head_size, 2, out_cols).sum(axis=1)
        row_squares = row_squares.transpose(1, 0, 2).reshape(2, width)
        out_w = lax.all_gather(out_part, "dp", axis=1, tiled=True)
        gate_w = lax.all_gather(gate_part, "dp", axis=1, tiled=True)
        out_w, down_part = lax.optimization_barrier((out_w, down_wide.astype(BF)))
        down_w = lax.all_gather(down_part, "dp", axis=1, tiled=True)

        x = tokens.astype(F32)
        h1 = (x * norm_scale(x) * attention_gain).astype(BF)
        cosine, sine = rotary_tables(rows)

        def squares_of(w):
            wide = w.astype(F32)
            return jnp.sum(wide * wide, axis=1)

        attn_n = jnp.sqrt(squares_of(attn_w) + NORM_EPS)
        attn_coef = attention_magnitude / attn_n
        z_attn = mm("tr,prc->ptc", h1, attn_w)
        projected = (z_attn * attn_coef[:, None, :]).reshape(3, rows, heads, HEAD_DIM)
        z_attn = z_attn.astype(BF)
        q = rotate(projected[0], cosine, sine).astype(BF)
        k = rotate(projected[1], cosine, sine).astype(BF)
        v = projected[2].astype(BF)

        row_n = jnp.sqrt(row_squares + NORM_EPS)
        out_n, down_n = row_n[0], row_n[1]
        out_coef = output_magnitude / out_n
        down_coef = downward_magnitude / down_n

        line = Line(head_size)
        spans = [slice(i * step_rows, (i + 1) * step_rows) for i in range(chunks)]
        attended, logs = [], []
        for i in range(chunks):
            a, l = attend_chunk(q, k, v, length, i * step_rows, step_rows)
            a = a.reshape(step_rows, attn_cols).astype(BF)
            attended.append(a)
            logs.append(l)
        for i in range(chunks):
            line.step(("out", i), mm("tr,rc->tc", attended[i], out_w).astype(BF))
        valid = (jnp.arange(rows) < length)[:, None]
        E = jnp.where(valid, cotangent.astype(F32), 0.0)
        gz_down = (E * down_coef).astype(BF)

        gate_n = jnp.sqrt(squares_of(gate_w) + NORM_EPS)
        gate_coef = gating_magnitude / gate_n

        kept = {n: [] for n in ("mid", "h2", "hid", "part", "gz", "c", "zout")}

        def feed_forward(i):
            s = spans[i]
            z_out = line.results[("out", i)].astype(F32)
            mid = x[s] + z_out * out_coef
            h2 = (mid * norm_scale(mid) * feedforward_gain).astype(BF)
            z = mm("tr,prc->ptc", h2, gate_w)
            g = z[0] * gate_coef[0]
            u = z[1] * gate_coef[1]
            sg = 1.0 / (1.0 + jnp.exp(-g))
            hid = (g * sg * u).astype(BF)
            part = mm("tr,rc->tc", hid, down_w).astype(BF)
            dh = mm("tc,rc->tr", gz_down[s], down_w)
            dg = dh * u * sg * (1.0 + g * (1.0 - sg))
            du = dh * g * sg
            c = jnp.stack([jnp.sum(z[0] * dg, axis=0), jnp.sum(z[1] * du, axis=0)])
            gz = jnp.stack([(dg * gate_coef[0]).astype(BF), (du * gate_coef[1]).astype(BF)])
            back = mm("tc,rc->tr", gz[0], gate_w[0]) + mm("tc,rc->tr", gz[1], gate_w[1])
            for n, val in (("mid", mid), ("h2", h2), ("hid", hid), ("part", part), ("gz", gz), ("c", c), ("zout", z_out)):
                kept[n].append(val)
            return back.astype(BF)

        fed = {}
        for i in range(chunks):
            while ("out", i) not in line.results:
                line.step()
            fed[i] = feed_forward(i)
            line.step(("mid", i), fed[i])
        for i in range(chunks):
            line.step(("down", i), kept["part"][i])
        grad_mid, grad_q, keys_grad, values_grad = [], [], 0.0, 0.0
        k_parts, v_parts = [0.0] * chunks, [0.0] * chunks
        gz_out, grad_att = [], []
        for i in range(chunks):
            s = spans[i]
            while ("mid", i) not in line.results:
                line.step()
            dh2 = line.results[("mid", i)].astype(F32)
            dm = E[s] + norm_back(kept["mid"][i], feedforward_gain, dh2)
            grad_mid.append(dm)
            go = (dm * out_coef).astype(BF)
            gz_out.append(go)
            ga = mm("tc,rc->tr", go, out_w).astype(BF)
            grad_att.append(ga)
            dq, dk, dv = attend_back_chunk(
                q, k, v, ga.reshape(step_rows, heads, HEAD_DIM), logs[i], length, i * step_rows, step_rows
            )
            grad_q.append(dq)
            for j in range(i + 1):
                k_parts[j] = k_parts[j] + dk[spans[j]]
                v_parts[j] = v_parts[j] + dv[spans[j]]
        dq = rotate_back(jnp.concatenate(grad_q, 0), cosine, sine)
        dk = rotate_back(jnp.concatenate(k_parts, 0), cosine, sine)
        dv = jnp.concatenate(v_parts, 0)
        g_attn = jnp.stack([dq, dk, dv]).reshape(3, rows, attn_cols)
        c_attn = jnp.sum(z_attn.astype(F32) * g_attn, axis=1)
        gz_attn = (g_attn * attn_coef[:, None, :]).astype(BF)
        for i in range(chunks):
            back = (
                mm("tc,rc->tr", gz_attn[0, spans[i]], attn_w[0])
                + mm("tc,rc->tr", gz_attn[1, spans[i]], attn_w[1])
                + mm("tc,rc->tr", gz_attn[2, spans[i]], attn_w[2])
            )
            line.step(("first", i), back.astype(BF))
        for i in range(3):
            line.step()

        def column_grads(h, gz, w, inner, outer, c, n, m):
            e = -c * m / (n * n * n)
            low = mm("ptc,pkc->ptk", gz, outer)
            d_inner = SCALE * (
                mm("ptk,td->pkd", low, h) + mm("pkc,pdc->pkd", outer * e[:, None, :], w)
            )
            red = mm("td,pdk->ptk", h, inner)
            d_outer = SCALE * (
                mm("ptk,ptc->pkc", red, gz) + mm("pdk,pdc->pkc", inner, w) * e[:, None, :]
            )
            return d_inner, d_outer, c / n

        def row_grads(h, gz, w, inner, outer, c, n, m):
            e = -c * m / (n * n * n)
            low = mm("tc,kc->tk", gz, outer)
            d_inner = SCALE * (mm("tk,tr->kr", low, h) + mm("kc,rc->kr", outer * e[None, :], w))
            red = mm("tr,rk->tk", h, inner)
            d_outer = SCALE * (mm("tk,tc->kc", red, gz) + mm("rk,rc->kc", inner, w) * e[None, :])
            return d_inner, d_outer, c / n

        h2 = jnp.concatenate(kept["h2"], 0)
        hid = jnp.concatenate(kept["hid"], 0)
        gz_gate = jnp.concatenate(kept["gz"], 1)
        gate_c = sum(kept["c"])
        gate_di, gate_do, gate_dm = column_grads(
            h2, gz_gate, gate_w, gating_inner, gating_outer, gate_c, gate_n, gating_magnitude
        )
        z_down = jnp.concatenate([line.results[("down", i)] for i in range(chunks)], 0).astype(F32)
        mid = jnp.concatenate(kept["mid"], 0)
        output = jnp.where(valid, mid + z_down * down_coef, 0.0).astype(BF)
        down_c = jnp.sum(z_down * E, axis=0)
        down_di, down_do, down_dm = row_grads(
            hid, gz_down, down_w, downward_inner, down_outer_factor, down_c, down_n, downward_magnitude
        )
        grad_middle = jnp.concatenate(grad_mid, 0)
        out_c = jnp.sum(jnp.concatenate(kept["zout"], 0) * grad_middle, axis=0)
        out_di, out_do, out_dm = row_grads(
            jnp.concatenate(attended, 0),
            jnp.concatenate(gz_out, 0),
            out_w,
            output_inner,
            output_outer_factor,
            out_c,
            out_n,
            output_magnitude,
        )
        attn_di, attn_do, attn_dm = column_grads(
            h1, gz_attn, attn_w, attention_inner, attention_outer, c_attn, attn_n, attention_magnitude
        )

        def low(*vals):
            return tuple(val.astype(BF) for val in vals)

        early = lax.psum(
            low(gate_di, gate_do, gate_dm, down_di, down_do, down_dm, out_di, out_do, out_dm), "dp"
        )
        gate_di, gate_do, gate_dm, down_di, down_do, down_dm, out_di, out_do, out_dm = early
        late = low(attn_di, attn_do, attn_dm)
        late, gate_di = lax.optimization_barrier((late, gate_di))
        attn_di, attn_do, attn_dm = lax.psum(late, "dp")
        gate_di, down_do, out_do, attn_di = lax.psum((gate_di, down_do, out_do, attn_di), "head")

        dh1 = jnp.concatenate([line.results[("first", i)] for i in range(chunks)], 0).astype(F32)
        grad_tokens = grad_middle + norm_back(x, attention_gain, dh1)

        def wide(val):
            return val.astype(F32)

        return (
            output,
            grad_tokens,
            wide(attn_di).transpose(0, 2, 1),
            wide(attn_do),
            wide(attn_dm),
            wide(out_di).T,
            wide(out_do),
            wide(out_dm),
            wide(gate_di).transpose(0, 2, 1),
            wide(gate_do),
            wide(gate_dm),
            wide(down_di).T,
            wide(down_do),
            wide(down_dm),
        )

    return on_device


def solution(mesh):
    return jax.shard_map(
        make(mesh),
        mesh=mesh,
        in_specs=(
            P("dp", None),
            P("dp", None),
            P("dp"),
            P(),
            P(),
            P(None, "dp", "head"),
            P("head", "dp"),
            P(None, "dp", "head"),
            P("head", "dp"),
            P(),
            P(None, None, "head"),
            P(None, "head"),
            P("head", None),
            P(),
            P(),
            P(),
            P(None, None, "head"),
            P(None, "head"),
            P("head", None),
            P(),
            P(),
        ),
        out_specs=(
            P("dp", None),
            P("dp", None),
            P(),
            P(None, None, "head"),
            P(None, "head"),
            P("head", None),
            P(),
            P(),
            P(),
            P(None, None, "head"),
            P(None, "head"),
            P("head", None),
            P(),
            P(),
        ),
        check_vma=False,
    )
```

```python
import jax
import jax.numpy as jnp
from jax import lax
from jax.experimental import pallas as pl
from jax.experimental.pallas import tpu as pltpu
from jax.sharding import PartitionSpec as P

HEAD_DIM = 128
SCALE = 2.0
EPS = 1e-05
NORM_EPS = 1e-06
NEG = -1e30
BF = jnp.bfloat16
F32 = jnp.float32


def mm(spec, a, b):
    return jnp.einsum(spec, a.astype(BF), b.astype(BF), preferred_element_type=F32)


def rotary_tables(total_rows):
    position = jnp.arange(total_rows).astype(F32)[:, None]
    inverse = 10000.0 ** (-jnp.arange(0, HEAD_DIM, 2).astype(F32) / HEAD_DIM)
    angles = position * inverse[None, :]
    angles = jnp.concatenate([angles, angles], axis=1)
    return jnp.cos(angles), jnp.sin(angles)


def norm_scale(values):
    return lax.rsqrt(jnp.mean(values * values, axis=-1, keepdims=True) + EPS)


def norm_back(values, gain, grad):
    r = norm_scale(values)
    a = gain * grad
    return r * a - values * (r * r * r) * jnp.mean(values * a, axis=-1, keepdims=True)


class Line:
    def __init__(self, size):
        self.size = size
        self.mid = None
        self.out = None
        self.queue = []
        self.results = {}

    def step(self, name=None, chunk=None):
        if self.size != 4:
            if chunk is not None:
                self.results[name] = lax.psum(chunk, "head")
            return
        new = None if chunk is None else (name, chunk)
        live = [v for v in (new, self.mid, self.out) if v is not None]
        if not live:
            return
        held = lax.optimization_barrier(tuple(v[1] for v in live))
        held = dict(zip([v[0] for v in live], held))
        index = lax.axis_index("head")
        end = (index == 0) | (index == 3)
        nxt_mid = nxt_out = None
        sent = {}
        if new is not None:
            sent["in"] = lax.ppermute(held[new[0]], "head", [(0, 1), (3, 2)])
        if self.mid is not None:
            sent["mid"] = lax.ppermute(held[self.mid[0]], "head", [(1, 2), (2, 1)])
        if self.out is not None:
            sent["out"] = lax.ppermute(held[self.out[0]], "head", [(1, 0), (2, 3)])
        keys = list(sent)
        sent = dict(zip(keys, lax.optimization_barrier(tuple(sent[k] for k in keys))))
        if self.out is not None:
            self.results[self.out[0]] = jnp.where(end, sent["out"], held[self.out[0]])
        if self.mid is not None:
            nxt_out = (self.mid[0], held[self.mid[0]] + sent["mid"])
        if new is not None:
            nxt_mid = (new[0], held[new[0]] + sent["in"])
        self.mid, self.out = nxt_mid, nxt_out


def turn(values, cosine, sine):
    return values * cosine + pltpu.roll(values, HEAD_DIM // 2, 1) * sine


def contract(left, right, ldim, rdim):
    return lax.dot_general(
        left, right, (((ldim,), (rdim,)), ((), ())), preferred_element_type=F32
    )


def masked_scores(qc, kk, length, offset):
    scores = contract(qc, kk, 1, 1) * HEAD_DIM ** (-0.5)
    row = offset + lax.broadcasted_iota(jnp.int32, scores.shape, 0)
    col = lax.broadcasted_iota(jnp.int32, scores.shape, 1)
    return jnp.where((col <= row) & (col < length), scores, NEG)


def forward_kernel(rows, len_ref, z_ref, coef_ref, cos_ref, sin_ref, qkv_ref, out_ref, log_ref):
    total = z_ref.shape[1]
    length = len_ref[0]
    for member in range(3):
        val = z_ref[member] * coef_ref[member : member + 1, :]
        if member < 2:
            val = turn(val, cos_ref[...], sin_ref[...])
        qkv_ref[member] = val.astype(BF)
    for offset in range(0, total, rows):
        keys = offset + rows
        scores = masked_scores(qkv_ref[0, offset:keys, :], qkv_ref[1, :keys, :], length, offset)
        top = jnp.max(scores, axis=1, keepdims=True)
        shifted = jnp.exp(scores - top)
        summed = jnp.sum(shifted, axis=1, keepdims=True)
        weights = (shifted * (1.0 / summed)).astype(BF)
        out_ref[offset:keys, :] = contract(weights, qkv_ref[2, :keys, :], 1, 0).astype(BF)
        log_ref[0, offset:keys, :] = top + jnp.log(summed)


def backward_kernel(
    rows, len_ref, qkv_ref, grad_ref, log_ref, coef_ref, cos_ref, sin_ref, gz_ref, c_ref, dq, dk, dv
):
    total = qkv_ref.shape[1]
    length = len_ref[0]
    factor = HEAD_DIM ** (-0.5)
    dk[...] = jnp.zeros_like(dk)
    dv[...] = jnp.zeros_like(dv)
    for offset in range(0, total, rows):
        keys = offset + rows
        qc = qkv_ref[0, offset:keys, :]
        grad = grad_ref[offset:keys, :]
        scores = masked_scores(qc, qkv_ref[1, :keys, :], length, offset)
        weights = jnp.exp(scores - log_ref[0, offset:keys, :])
        dv[:keys, :] += contract(weights.astype(BF), grad, 0, 0)
        dw = contract(grad, qkv_ref[2, :keys, :], 1, 1)
        mean = jnp.sum(weights * dw, axis=1, keepdims=True)
        ds = (weights * (dw - mean)).astype(BF)
        dq[offset:keys, :] = contract(ds, qkv_ref[1, :keys, :], 1, 0) * factor
        dk[:keys, :] += contract(ds, qc, 0, 0)
    for member, acc in enumerate((dq, dk, dv)):
        grads = acc[...]
        unturned = qkv_ref[member].astype(F32)
        if member == 1:
            grads = grads * factor
        if member < 2:
            grads = turn(grads, cos_ref[...], -sin_ref[...])
            unturned = turn(unturned, cos_ref[...], -sin_ref[...])
        coef = coef_ref[member : member + 1, :]
        gz_ref[member] = (grads * coef).astype(BF)
        c_ref[member : member + 1, :] = jnp.sum(unturned * grads, axis=0, keepdims=True) / coef


def head_specs(total):
    three = pl.BlockSpec((3, total, HEAD_DIM), lambda h: (0, 0, h))
    flat = pl.BlockSpec((total, HEAD_DIM), lambda h: (0, h))
    small = pl.BlockSpec((3, HEAD_DIM), lambda h: (0, h))
    table = pl.BlockSpec((total, HEAD_DIM), lambda h: (0, 0))
    log = pl.BlockSpec((1, total, 1), lambda h: (h, 0, 0))
    scalar = pl.BlockSpec(memory_space=pltpu.SMEM)
    return three, flat, small, table, log, scalar


def attend(lengths, z, coef, cosine, sine, rows):
    total, cols = z.shape[1:]
    three, flat, small, table, log, scalar = head_specs(total)
    heads = cols // HEAD_DIM
    return pl.pallas_call(
        lambda *refs: forward_kernel(rows, *refs),
        grid=(heads,),
        in_specs=[scalar, three, small, table, table],
        out_specs=[three, flat, log],
        out_shape=[
            jax.ShapeDtypeStruct(z.shape, BF),
            jax.ShapeDtypeStruct((total, cols), BF),
            jax.ShapeDtypeStruct((heads, total, 1), F32),
        ],
        cost_estimate=pl.CostEstimate(
            flops=4 * total * total * cols, bytes_accessed=20 * total * cols, transcendentals=total * total * heads
        ),
        name="attend_forward",
    )(lengths, z, coef, cosine, sine)


def attend_back(lengths, qkv, grad, logs, coef, cosine, sine, rows):
    total, cols = qkv.shape[1:]
    three, flat, small, table, log, scalar = head_specs(total)
    heads = cols // HEAD_DIM
    return pl.pallas_call(
        lambda *refs: backward_kernel(rows, *refs),
        grid=(heads,),
        in_specs=[scalar, three, flat, log, small, table, table],
        out_specs=[three, small],
        out_shape=[jax.ShapeDtypeStruct(qkv.shape, BF), jax.ShapeDtypeStruct((3, cols), F32)],
        scratch_shapes=[pltpu.VMEM((total, HEAD_DIM), F32)] * 3,
        cost_estimate=pl.CostEstimate(
            flops=10 * total * total * cols, bytes_accessed=14 * total * cols, transcendentals=total * total * heads
        ),
        name="attend_backward",
    )(lengths, qkv, grad, logs, coef, cosine, sine)


def butterfly(val, axis, size):
    hop = 1
    while hop < size:
        val = val + lax.ppermute(val, axis, [(i, i ^ hop) for i in range(size)])
        hop *= 2
    return val


def make(mesh):
    head_size = mesh.shape["head"]
    dp_size = mesh.shape["dp"]

    def on_device(
        tokens,
        cotangent,
        lengths,
        attention_gain,
        feedforward_gain,
        attention_base,
        output_base,
        gating_base,
        downward_base,
        attention_inner,
        attention_outer,
        attention_magnitude,
        output_inner,
        output_outer_factor,
        output_magnitude,
        gating_inner,
        gating_outer,
        gating_magnitude,
        downward_inner,
        down_outer_factor,
        downward_magnitude,
    ):
        rows, width = tokens.shape
        length = lengths[0]
        dp = lax.axis_index("dp")
        in_rows = attention_base.shape[1]
        out_cols = output_base.shape[1]
        attn_cols = attention_base.shape[2]
        gate_cols = gating_base.shape[2]
        heads = attn_cols // HEAD_DIM
        step_rows = min(256, rows)
        chunks = rows // step_rows

        def merge_column(base, inner, outer):
            part = lax.dynamic_slice_in_dim(inner, dp * in_rows, in_rows, axis=1)
            low = mm("prk,pkc->prc", part, outer)
            return base.astype(F32) + SCALE * low

        def merge_row(base, inner, outer):
            part = lax.dynamic_slice_in_dim(outer, dp * out_cols, out_cols, axis=1)
            return base.astype(F32) + SCALE * mm("rk,kc->rc", inner, part)

        attn_part = merge_column(attention_base, attention_inner, attention_outer).astype(BF)
        out_wide = merge_row(output_base, output_inner, output_outer_factor)
        first_part = jnp.concatenate([attn_part, out_wide.astype(BF).T[None]], 0)
        first_w = lax.all_gather(first_part, "dp", axis=1, tiled=True)
        attn_w, out_w = first_w[:3], first_w[3]
        down_wide = merge_row(downward_base, downward_inner, down_outer_factor)
        gate_part = merge_column(gating_base, gating_inner, gating_outer).astype(BF)
        second_part = jnp.concatenate([gate_part, down_wide.astype(BF).T[None]], 0)
        first_w, second_part = lax.optimization_barrier((first_w, second_part))
        attn_w, out_w = first_w[:3], first_w[3]
        second_w = lax.all_gather(second_part, "dp", axis=1, tiled=True)
        gate_w, down_w = second_w[:2], second_w[2]
        row_squares = jnp.stack(
            [jnp.sum(out_wide * out_wide, axis=0), jnp.sum(down_wide * down_wide, axis=0)]
        )
        slots = (jnp.arange(dp_size) == dp).astype(F32)[None, :, None] * row_squares[:, None, :]
        slots = butterfly(butterfly(slots, "head", head_size), "dp", dp_size)
        row_squares = slots.reshape(2, width)

        x = tokens.astype(F32)
        h1 = (x * norm_scale(x) * attention_gain).astype(BF)
        cosine, sine = rotary_tables(rows)
        sine = jnp.where(jnp.arange(HEAD_DIM) < HEAD_DIM // 2, -sine, sine)

        def squares_of(w):
            wide = w.astype(F32)
            return jnp.sum(wide * wide, axis=1)

        attn_n = jnp.sqrt(squares_of(attn_w) + NORM_EPS)
        attn_coef = attention_magnitude / attn_n
        z_attn = mm("tr,prc->ptc", h1, attn_w)
        qkv, attended, logs = attend(lengths, z_attn, attn_coef, cosine, sine, step_rows)

        row_n = jnp.sqrt(row_squares + NORM_EPS)
        out_n, down_n = row_n[0], row_n[1]
        out_coef = output_magnitude / out_n
        down_coef = downward_magnitude / down_n

        line = Line(head_size)
        spans = [slice(i * step_rows, (i + 1) * step_rows) for i in range(chunks)]
        for i in range(chunks):
            line.step(("out", i), mm("tr,cr->tc", attended[spans[i]], out_w).astype(BF))
        valid = (jnp.arange(rows) < length)[:, None]
        E = jnp.where(valid, cotangent.astype(F32), 0.0)
        gz_down = (E * down_coef).astype(BF)

        gate_n = jnp.sqrt(squares_of(gate_w) + NORM_EPS)
        gate_coef = gating_magnitude / gate_n

        gate_inner = gating_inner.transpose(1, 0, 2).reshape(width, -1)
        gate_inner = jnp.concatenate([gate_inner, jnp.zeros((width, 128 - gate_inner.shape[1]), F32)], 1).astype(BF)
        kept = {n: [] for n in ("mid", "part", "c", "gate_di", "gate_do", "down_di", "down_do", "out_di", "out_do", "out_c")}
        rank = gating_inner.shape[2]

        def row_parts(h, gz, inner, outer):
            low = mm("tc,kc->tk", gz, outer)
            red = mm("tr,rk->tk", h, inner)
            return mm("tk,tr->kr", low, h), mm("tk,tc->kc", red, gz)

        def feed_forward(i):
            s = spans[i]
            z_out = line.results[("out", i)].astype(F32)
            mid = x[s] + z_out * out_coef
            h2 = (mid * norm_scale(mid) * feedforward_gain).astype(BF)
            z = mm("tr,prc->ptc", h2, gate_w)
            g = z[0] * gate_coef[0]
            u = z[1] * gate_coef[1]
            sg = 1.0 / (1.0 + jnp.exp(-g))
            hid = (g * sg * u).astype(BF)
            part = mm("tr,cr->tc", hid, down_w).astype(BF)
            dh = mm("tc,cr->tr", gz_down[s], down_w)
            dg = dh * u * sg * (1.0 + g * (1.0 - sg))
            du = dh * g * sg
            c = jnp.stack([jnp.sum(z[0] * dg, axis=0), jnp.sum(z[1] * du, axis=0)])
            gz = jnp.stack([(dg * gate_coef[0]).astype(BF), (du * gate_coef[1]).astype(BF)])
            back = mm("tc,rc->tr", gz[0], gate_w[0]) + mm("tc,rc->tr", gz[1], gate_w[1])
            low = jnp.concatenate([mm("tc,kc->tk", gz[p], gating_outer[p]) for p in range(2)], 1)
            red = mm("tr,rk->tk", h2, gate_inner)
            d_inner = mm("tk,td->kd", low, h2).reshape(2, rank, width)
            d_outer = jnp.stack(
                [mm("tk,tc->kc", red[:, p * rank : (p + 1) * rank], gz[p]) for p in range(2)]
            )
            down_di, down_do = row_parts(hid, gz_down[s], downward_inner, down_outer_factor)
            for n, val in (
                ("mid", (mid, z_out)),
                ("part", part),
                ("c", c),
                ("gate_di", d_inner),
                ("gate_do", d_outer),
                ("down_di", down_di),
                ("down_do", down_do),
            ):
                kept[n].append(val)
            return back.astype(BF)

        fed = {}
        for i in range(chunks):
            while ("out", i) not in line.results:
                line.step()
            fed[i] = feed_forward(i)
            line.step(("mid", i), fed[i])
        for i in range(chunks):
            line.step(("down", i), kept["part"][i])
        def column_end(d_inner, d_outer, w, inner, outer, c, n, m):
            e = -c * m / (n * n * n)
            d_inner = SCALE * (d_inner + mm("pkc,pdc->pkd", outer * e[:, None, :], w))
            d_outer = SCALE * (d_outer + mm("pdk,pdc->pkc", inner, w) * e[:, None, :])
            return d_inner, d_outer, c / n

        def row_end(d_inner, d_outer, w, inner, outer, c, n, m):
            e = -c * m / (n * n * n)
            d_inner = SCALE * (d_inner + mm("kc,cr->kr", outer * e[None, :], w))
            d_outer = SCALE * (d_outer + mm("rk,cr->kc", inner, w) * e[None, :])
            return d_inner, d_outer, c / n

        def low(*vals):
            return tuple(val.astype(BF) for val in vals)

        gate_di, gate_do, gate_dm = column_end(
            sum(kept["gate_di"]), sum(kept["gate_do"]), gate_w, gating_inner, gating_outer,
            sum(kept["c"]), gate_n, gating_magnitude,
        )
        gate_di, gate_do, gate_dm = lax.psum(low(gate_di, gate_do, gate_dm), "dp")
        gate_di = lax.psum(gate_di, "head")

        grad_mid, grad_att = [], []
        for i in range(chunks):
            s = spans[i]
            while ("mid", i) not in line.results:
                line.step()
            dh2 = line.results[("mid", i)].astype(F32)
            mid, z_out = kept["mid"][i]
            dm = E[s] + norm_back(mid, feedforward_gain, dh2)
            grad_mid.append(dm)
            go = (dm * out_coef).astype(BF)
            grad_att.append(mm("tc,cr->tr", go, out_w).astype(BF))
            kept["out_c"].append(jnp.sum(z_out * dm, axis=0))
            out_di, out_do = row_parts(attended[s], go, output_inner, output_outer_factor)
            kept["out_di"].append(out_di)
            kept["out_do"].append(out_do)
        gz_attn, c_attn = attend_back(
            lengths, qkv, jnp.concatenate(grad_att, 0), logs, attn_coef, cosine, sine, step_rows
        )
        for i in range(chunks):
            back = (
                mm("tc,rc->tr", gz_attn[0, spans[i]], attn_w[0])
                + mm("tc,rc->tr", gz_attn[1, spans[i]], attn_w[1])
                + mm("tc,rc->tr", gz_attn[2, spans[i]], attn_w[2])
            )
            line.step(("first", i), back.astype(BF))
        for i in range(3):
            line.step()

        outputs, down_c = [], 0.0
        for i in range(chunks):
            z_down = line.results[("down", i)].astype(F32)
            s = spans[i]
            outputs.append(jnp.where(valid[s], kept["mid"][i][0] + z_down * down_coef, 0.0).astype(BF))
            down_c = down_c + jnp.sum(z_down * E[s], axis=0)
        output = jnp.concatenate(outputs, 0)
        out_di, out_do, out_dm = row_end(
            sum(kept["out_di"]), sum(kept["out_do"]), out_w, output_inner, output_outer_factor,
            sum(kept["out_c"]), out_n, output_magnitude,
        )
        down_di, down_do, down_dm = row_end(
            sum(kept["down_di"]), sum(kept["down_do"]), down_w, downward_inner, down_outer_factor,
            down_c, down_n, downward_magnitude,
        )
        attn_low = mm("ptc,pkc->ptk", gz_attn, attention_outer)
        attn_red = mm("td,pdk->ptk", h1, attention_inner)
        attn_di, attn_do, attn_dm = column_end(
            mm("ptk,td->pkd", attn_low, h1), mm("ptk,ptc->pkc", attn_red, gz_attn), attn_w,
            attention_inner, attention_outer, c_attn, attn_n, attention_magnitude,
        )

        def over_dp(val):
            return butterfly(val.astype(BF), "dp", dp_size)

        wide_set = [attn_di.reshape(3 * rank, width), out_do, down_do]
        wide_set = jnp.concatenate(wide_set, 0)
        wide_set = butterfly(over_dp(wide_set), "head", head_size)
        attn_di = wide_set[: 3 * rank].reshape(3, rank, width)
        out_do, down_do = wide_set[3 * rank : 4 * rank], wide_set[4 * rank :]
        narrow = over_dp(jnp.concatenate([attn_do.reshape(3 * rank, -1), attn_dm, out_di], 0))
        attn_do = narrow[: 3 * rank].reshape(3, rank, -1)
        attn_dm = narrow[3 * rank : 3 * rank + 3]
        out_di = narrow[3 * rank + 3 :]
        down_di = over_dp(down_di)
        mags = over_dp(jnp.stack([out_dm, down_dm]))
        out_dm, down_dm = mags[0], mags[1]

        first = jnp.concatenate([line.results[("first", i)] for i in range(chunks)], 0).astype(F32)
        grad_tokens = jnp.concatenate(grad_mid, 0) + norm_back(x, attention_gain, first)

        def wide(val):
            return val.astype(F32)

        return (
            output,
            grad_tokens,
            wide(attn_di).transpose(0, 2, 1),
            wide(attn_do),
            wide(attn_dm),
            wide(out_di).T,
            wide(out_do),
            wide(out_dm),
            wide(gate_di).transpose(0, 2, 1),
            wide(gate_do),
            wide(gate_dm),
            wide(down_di).T,
            wide(down_do),
            wide(down_dm),
        )

    return on_device


def solution(mesh):
    return jax.shard_map(
        make(mesh),
        mesh=mesh,
        in_specs=(
            P("dp", None),
            P("dp", None),
            P("dp"),
            P(),
            P(),
            P(None, "dp", "head"),
            P("head", "dp"),
            P(None, "dp", "head"),
            P("head", "dp"),
            P(),
            P(None, None, "head"),
            P(None, "head"),
            P("head", None),
            P(),
            P(),
            P(),
            P(None, None, "head"),
            P(None, "head"),
            P("head", None),
            P(),
            P(),
        ),
        out_specs=(
            P("dp", None),
            P("dp", None),
            P(),
            P(None, None, "head"),
            P(None, "head"),
            P("head", None),
            P(),
            P(),
            P(),
            P(None, None, "head"),
            P(None, "head"),
            P("head", None),
            P(),
            P(),
        ),
        check_vma=False,
    )
```

```python
import jax
import jax.numpy as jnp
from jax import lax
from jax.experimental import pallas as pl
from jax.experimental.pallas import tpu as pltpu
from jax.sharding import PartitionSpec as P

HEAD_DIM = 128
SCALE = 2.0
EPS = 1e-05
NORM_EPS = 1e-06
NEG = -1e30
BF = jnp.bfloat16
F32 = jnp.float32


def mm(spec, a, b):
    return jnp.einsum(spec, a.astype(BF), b.astype(BF), preferred_element_type=F32)


def rotary_tables(total_rows):
    position = jnp.arange(total_rows).astype(F32)[:, None]
    inverse = 10000.0 ** (-jnp.arange(0, HEAD_DIM, 2).astype(F32) / HEAD_DIM)
    angles = position * inverse[None, :]
    angles = jnp.concatenate([angles, angles], axis=1)
    return jnp.cos(angles), jnp.sin(angles)


def norm_scale(values):
    return lax.rsqrt(jnp.mean(values * values, axis=-1, keepdims=True) + EPS)


def norm_back(values, gain, grad):
    r = norm_scale(values)
    a = gain * grad
    return r * a - values * (r * r * r) * jnp.mean(values * a, axis=-1, keepdims=True)


class Line:
    def __init__(self, size):
        self.size = size
        self.mid = None
        self.out = None
        self.queue = []
        self.results = {}

    def step(self, name=None, chunk=None):
        if self.size != 4:
            if chunk is not None:
                self.results[name] = lax.psum(chunk, "head")
            return
        new = None if chunk is None else (name, chunk)
        live = [v for v in (new, self.mid, self.out) if v is not None]
        if not live:
            return
        held = lax.optimization_barrier(tuple(v[1] for v in live))
        held = dict(zip([v[0] for v in live], held))
        index = lax.axis_index("head")
        end = (index == 0) | (index == 3)
        nxt_mid = nxt_out = None
        sent = {}
        if new is not None:
            sent["in"] = lax.ppermute(held[new[0]], "head", [(0, 1), (3, 2)])
        if self.mid is not None:
            sent["mid"] = lax.ppermute(held[self.mid[0]], "head", [(1, 2), (2, 1)])
        if self.out is not None:
            sent["out"] = lax.ppermute(held[self.out[0]], "head", [(1, 0), (2, 3)])
        keys = list(sent)
        sent = dict(zip(keys, lax.optimization_barrier(tuple(sent[k] for k in keys))))
        if self.out is not None:
            self.results[self.out[0]] = jnp.where(end, sent["out"], held[self.out[0]])
        if self.mid is not None:
            nxt_out = (self.mid[0], held[self.mid[0]] + sent["mid"])
        if new is not None:
            nxt_mid = (new[0], held[new[0]] + sent["in"])
        self.mid, self.out = nxt_mid, nxt_out


def turn(values, cosine, sine):
    return values * cosine + pltpu.roll(values, HEAD_DIM // 2, 1) * sine


def contract(left, right, ldim, rdim):
    return lax.dot_general(
        left, right, (((ldim,), (rdim,)), ((), ())), preferred_element_type=F32
    )


def masked_scores(qc, kk, length, offset):
    scores = contract(qc, kk, 1, 1) * HEAD_DIM ** (-0.5)
    row = offset + lax.broadcasted_iota(jnp.int32, scores.shape, 0)
    col = lax.broadcasted_iota(jnp.int32, scores.shape, 1)
    return jnp.where((col <= row) & (col < length), scores, NEG)


def forward_kernel(rows, len_ref, z_ref, coef_ref, cos_ref, sin_ref, qkv_ref, out_ref, log_ref):
    total = z_ref.shape[1]
    length = len_ref[0]
    for member in range(3):
        val = z_ref[member] * coef_ref[member : member + 1, :]
        if member < 2:
            val = turn(val, cos_ref[...], sin_ref[...])
        qkv_ref[member] = val.astype(BF)
    for offset in range(0, total, rows):
        keys = offset + rows
        scores = masked_scores(qkv_ref[0, offset:keys, :], qkv_ref[1, :keys, :], length, offset)
        top = jnp.max(scores, axis=1, keepdims=True)
        shifted = jnp.exp(scores - top)
        summed = jnp.sum(shifted, axis=1, keepdims=True)
        weights = (shifted * (1.0 / summed)).astype(BF)
        out_ref[offset:keys, :] = contract(weights, qkv_ref[2, :keys, :], 1, 0).astype(BF)
        log_ref[0, offset:keys, :] = top + jnp.log(summed)


def backward_kernel(
    rows, len_ref, qkv_ref, grad_ref, log_ref, coef_ref, cos_ref, sin_ref, gz_ref, c_ref, dq, dk, dv
):
    total = qkv_ref.shape[1]
    length = len_ref[0]
    factor = HEAD_DIM ** (-0.5)
    dk[...] = jnp.zeros_like(dk)
    dv[...] = jnp.zeros_like(dv)
    for offset in range(0, total, rows):
        keys = offset + rows
        qc = qkv_ref[0, offset:keys, :]
        grad = grad_ref[offset:keys, :]
        scores = masked_scores(qc, qkv_ref[1, :keys, :], length, offset)
        weights = jnp.exp(scores - log_ref[0, offset:keys, :])
        dv[:keys, :] += contract(weights.astype(BF), grad, 0, 0)
        dw = contract(grad, qkv_ref[2, :keys, :], 1, 1)
        mean = jnp.sum(weights * dw, axis=1, keepdims=True)
        ds = (weights * (dw - mean)).astype(BF)
        dq[offset:keys, :] = contract(ds, qkv_ref[1, :keys, :], 1, 0) * factor
        dk[:keys, :] += contract(ds, qc, 0, 0)
    for member, acc in enumerate((dq, dk, dv)):
        grads = acc[...]
        unturned = qkv_ref[member].astype(F32)
        if member == 1:
            grads = grads * factor
        if member < 2:
            grads = turn(grads, cos_ref[...], -sin_ref[...])
            unturned = turn(unturned, cos_ref[...], -sin_ref[...])
        coef = coef_ref[member : member + 1, :]
        gz_ref[member] = (grads * coef).astype(BF)
        c_ref[member : member + 1, :] = jnp.sum(unturned * grads, axis=0, keepdims=True) / coef


def head_specs(total):
    three = pl.BlockSpec((3, total, HEAD_DIM), lambda h: (0, 0, h))
    flat = pl.BlockSpec((total, HEAD_DIM), lambda h: (0, h))
    small = pl.BlockSpec((3, HEAD_DIM), lambda h: (0, h))
    table = pl.BlockSpec((total, HEAD_DIM), lambda h: (0, 0))
    log = pl.BlockSpec((1, total, 1), lambda h: (h, 0, 0))
    scalar = pl.BlockSpec(memory_space=pltpu.SMEM)
    return three, flat, small, table, log, scalar


def attend(lengths, z, coef, cosine, sine, rows):
    total, cols = z.shape[1:]
    three, flat, small, table, log, scalar = head_specs(total)
    heads = cols // HEAD_DIM
    return pl.pallas_call(
        lambda *refs: forward_kernel(rows, *refs),
        grid=(heads,),
        in_specs=[scalar, three, small, table, table],
        out_specs=[three, flat, log],
        out_shape=[
            jax.ShapeDtypeStruct(z.shape, BF),
            jax.ShapeDtypeStruct((total, cols), BF),
            jax.ShapeDtypeStruct((heads, total, 1), F32),
        ],
        cost_estimate=pl.CostEstimate(
            flops=4 * total * total * cols, bytes_accessed=20 * total * cols, transcendentals=total * total * heads
        ),
        name="attend_forward",
    )(lengths, z, coef, cosine, sine)


def attend_back(lengths, qkv, grad, logs, coef, cosine, sine, rows):
    total, cols = qkv.shape[1:]
    three, flat, small, table, log, scalar = head_specs(total)
    heads = cols // HEAD_DIM
    return pl.pallas_call(
        lambda *refs: backward_kernel(rows, *refs),
        grid=(heads,),
        in_specs=[scalar, three, flat, log, small, table, table],
        out_specs=[three, small],
        out_shape=[jax.ShapeDtypeStruct(qkv.shape, BF), jax.ShapeDtypeStruct((3, cols), F32)],
        scratch_shapes=[pltpu.VMEM((total, HEAD_DIM), F32)] * 3,
        cost_estimate=pl.CostEstimate(
            flops=10 * total * total * cols, bytes_accessed=14 * total * cols, transcendentals=total * total * heads
        ),
        name="attend_backward",
    )(lengths, qkv, grad, logs, coef, cosine, sine)


def chained(kernel, grid, in_specs, args, outs, previous, flops, moved, name):
    held = [(pos, previous[pos]) for pos in sorted(previous)]
    count = len(args)

    def body(*refs):
        kernel(*refs[:count], *refs[count + len(held) :])

    return pl.pallas_call(
        body,
        grid=grid,
        in_specs=list(in_specs) + [pl.BlockSpec(memory_space=pl.ANY)] * len(held),
        out_specs=[o[1] for o in outs],
        out_shape=[o[0] for o in outs],
        input_output_aliases={count + n: pos for n, (pos, _) in enumerate(held)},
        scratch_shapes=outs_scratch(name, outs),
        cost_estimate=pl.CostEstimate(flops=flops, bytes_accessed=moved, transcendentals=0),
        name=name,
    )(*args, *[v for _, v in held])


def outs_scratch(name, outs):
    if name != "feed_forward":
        return []
    block = outs[1][1].block_shape
    return [pltpu.VMEM(block, F32), pltpu.VMEM(block, F32)]


def feed_kernel(
    x_ref, zo_ref, ocoef_ref, gain_ref, gzd_ref, w_ref, coef_ref,
    mid_ref, h2_ref, hid_ref, gz_ref, c_ref, part_ref, back_ref, cd_ref, acc_part, acc_back,
):
    step = pl.program_id(0)

    @pl.when(step == 0)
    def _():
        mid = x_ref[...].astype(F32) + zo_ref[...].astype(F32) * ocoef_ref[...]
        mid_ref[...] = mid
        h2_ref[...] = (mid * norm_scale(mid) * gain_ref[...]).astype(BF)
        acc_part[...] = jnp.zeros_like(acc_part)
        acc_back[...] = jnp.zeros_like(acc_back)

    h2 = h2_ref[...]
    zg = contract(h2, w_ref[0], 1, 0)
    zu = contract(h2, w_ref[1], 1, 0)
    dh = contract(gzd_ref[...], w_ref[2], 1, 0)
    cg, cu = coef_ref[0:1, :], coef_ref[1:2, :]
    g, u = zg * cg, zu * cu
    sg = 1.0 / (1.0 + jnp.exp(-g))
    hid = (g * sg * u).astype(BF)
    dg = dh * u * sg * (1.0 + g * (1.0 - sg))
    du = dh * g * sg
    c_ref[0:1, :] = jnp.sum(zg * dg, axis=0, keepdims=True)
    c_ref[1:2, :] = jnp.sum(zu * du, axis=0, keepdims=True)
    gg, gu = (dg * cg).astype(BF), (du * cu).astype(BF)
    gz_ref[0] = gg
    gz_ref[1] = gu
    hid_ref[...] = hid
    acc_part[...] += contract(hid, w_ref[2], 1, 1)
    both = jnp.concatenate([w_ref[0], w_ref[1]], axis=1)
    acc_back[...] += contract(jnp.concatenate([gg, gu], axis=1), both, 1, 1)

    @pl.when(step == pl.num_programs(0) - 1)
    def _():
        part = acc_part[...]
        part_ref[...] = part.astype(BF)
        back_ref[...] = acc_back[...].astype(BF)
        cd_ref[...] = jnp.sum(part * gzd_ref[...].astype(F32), axis=0, keepdims=True)


def valid_rows(length, offset, shape):
    return offset + lax.broadcasted_iota(jnp.int32, shape, 0) < length


def middle_kernel(
    offset, len_ref, z_ref, mid_ref, zo_ref, cot_ref, gain_ref, ocoef_ref, w_ref, dm_ref, go_ref, ga_ref, c_ref
):
    valid = valid_rows(len_ref[0], offset, cot_ref.shape)
    grad = jnp.where(valid, cot_ref[...].astype(F32), 0.0)
    dm = grad + norm_back(mid_ref[...], gain_ref[...], z_ref[...].astype(F32))
    dm_ref[...] = dm
    go = (dm * ocoef_ref[...]).astype(BF)
    go_ref[...] = go
    ga_ref[...] = contract(go, w_ref[0], 1, 0).astype(BF)
    c_ref[...] = jnp.sum(zo_ref[...].astype(F32) * dm, axis=0, keepdims=True)


def output_kernel(offset, len_ref, z_ref, mid_ref, coef_ref, out_ref):
    valid = valid_rows(len_ref[0], offset, mid_ref.shape)
    val = mid_ref[...] + z_ref[...].astype(F32) * coef_ref[...]
    out_ref[...] = jnp.where(valid, val, 0.0).astype(BF)


def tokens_kernel(z_ref, x_ref, dm_ref, gain_ref, out_ref):
    out_ref[...] = dm_ref[...] + norm_back(
        x_ref[...].astype(F32), gain_ref[...], z_ref[...].astype(F32)
    )


def butterfly(val, axis, size):
    hop = 1
    while hop < size:
        val = val + lax.ppermute(val, axis, [(i, i ^ hop) for i in range(size)])
        hop *= 2
    return val


def make(mesh):
    head_size = mesh.shape["head"]
    dp_size = mesh.shape["dp"]

    def on_device(
        tokens,
        cotangent,
        lengths,
        attention_gain,
        feedforward_gain,
        attention_base,
        output_base,
        gating_base,
        downward_base,
        attention_inner,
        attention_outer,
        attention_magnitude,
        output_inner,
        output_outer_factor,
        output_magnitude,
        gating_inner,
        gating_outer,
        gating_magnitude,
        downward_inner,
        down_outer_factor,
        downward_magnitude,
    ):
        rows, width = tokens.shape
        length = lengths[0]
        dp = lax.axis_index("dp")
        in_rows = attention_base.shape[1]
        out_cols = output_base.shape[1]
        attn_cols = attention_base.shape[2]
        gate_cols = gating_base.shape[2]
        heads = attn_cols // HEAD_DIM
        step_rows = min(256, rows)
        chunks = rows // step_rows

        def merge_column(base, inner, outer):
            part = lax.dynamic_slice_in_dim(inner, dp * in_rows, in_rows, axis=1)
            low = mm("prk,pkc->prc", part, outer)
            return base.astype(F32) + SCALE * low

        def merge_row(base, inner, outer):
            part = lax.dynamic_slice_in_dim(outer, dp * out_cols, out_cols, axis=1)
            return base.astype(F32) + SCALE * mm("rk,kc->rc", inner, part)

        attn_part = merge_column(attention_base, attention_inner, attention_outer).astype(BF)
        out_wide = merge_row(output_base, output_inner, output_outer_factor)
        first_part = jnp.concatenate([attn_part, out_wide.astype(BF).T[None]], 0)
        first_w = lax.all_gather(first_part, "dp", axis=1, tiled=True)
        attn_w, out_w = first_w[:3], first_w[3]
        down_wide = merge_row(downward_base, downward_inner, down_outer_factor)
        gate_part = merge_column(gating_base, gating_inner, gating_outer).astype(BF)
        second_part = jnp.concatenate([gate_part, down_wide.astype(BF).T[None]], 0)
        first_w, second_part = lax.optimization_barrier((first_w, second_part))
        attn_w, out_w = first_w[:3], first_w[3]
        second_w = lax.all_gather(second_part, "dp", axis=1, tiled=True)
        gate_w, down_w = second_w[:2], second_w[2]
        row_squares = jnp.stack(
            [jnp.sum(out_wide * out_wide, axis=0), jnp.sum(down_wide * down_wide, axis=0)]
        )
        slots = (jnp.arange(dp_size) == dp).astype(F32)[None, :, None] * row_squares[:, None, :]
        slots = butterfly(butterfly(slots, "head", head_size), "dp", dp_size)
        row_squares = slots.reshape(2, width)

        x = tokens.astype(F32)
        h1 = (x * norm_scale(x) * attention_gain).astype(BF)
        cosine, sine = rotary_tables(rows)
        sine = jnp.where(jnp.arange(HEAD_DIM) < HEAD_DIM // 2, -sine, sine)

        def squares_of(w):
            wide = w.astype(F32)
            return jnp.sum(wide * wide, axis=1)

        attn_n = jnp.sqrt(squares_of(attn_w) + NORM_EPS)
        attn_coef = attention_magnitude / attn_n
        z_attn = mm("tr,prc->ptc", h1, attn_w)
        qkv, attended, logs = attend(lengths, z_attn, attn_coef, cosine, sine, step_rows)

        row_n = jnp.sqrt(row_squares + NORM_EPS)
        out_n, down_n = row_n[0], row_n[1]
        out_coef = output_magnitude / out_n
        down_coef = downward_magnitude / down_n

        line = Line(head_size)
        spans = [slice(i * step_rows, (i + 1) * step_rows) for i in range(chunks)]
        for i in range(chunks):
            line.step(("out", i), mm("tr,cr->tc", attended[spans[i]], out_w).astype(BF))
        valid = (jnp.arange(rows) < length)[:, None]
        gz_down = (jnp.where(valid, cotangent.astype(F32), 0.0) * down_coef).astype(BF)

        gate_n = jnp.sqrt(squares_of(gate_w) + NORM_EPS)
        gate_coef = gating_magnitude / gate_n
        rank = gating_inner.shape[2]

        def flat(n):
            return pl.BlockSpec((step_rows, n), lambda *g: (0, 0))

        def at(i, n):
            return pl.BlockSpec((step_rows, n), lambda *g: (i, 0))

        def vec(n):
            return pl.BlockSpec((1, n), lambda *g: (0, 0))

        def shape(dims, dtype):
            return jax.ShapeDtypeStruct(dims, dtype)

        smem = pl.BlockSpec(memory_space=pltpu.SMEM)
        lanes = 128
        blocks = gate_cols // lanes
        full = {}

        def feed_forward(i):
            outs = [
                (shape((rows, width), F32), at(i, width)),
                (shape((rows, width), BF), at(i, width)),
                (shape((rows, gate_cols), BF), pl.BlockSpec((step_rows, lanes), lambda j: (i, j))),
                (shape((2, rows, gate_cols), BF), pl.BlockSpec((2, step_rows, lanes), lambda j: (0, i, j))),
                (shape((2, gate_cols), F32), pl.BlockSpec((2, lanes), lambda j: (0, j))),
                (shape((step_rows, width), BF), flat(width)),
                (shape((step_rows, width), BF), flat(width)),
                (shape((1, width), F32), vec(width)),
            ]
            mid, h2, hid, gz, c, part, back, cd = chained(
                feed_kernel,
                (blocks,),
                [
                    at(i, width), flat(width), vec(width), vec(width), at(i, width),
                    pl.BlockSpec((3, width, lanes), lambda j: (0, 0, j)),
                    pl.BlockSpec((2, lanes), lambda j: (0, j)),
                ],
                [tokens, line.results[("out", i)], out_coef[None], feedforward_gain[None], gz_down, second_w, gate_coef],
                outs,
                {n: full[n] for n in full},
                12 * step_rows * width * gate_cols,
                6 * width * gate_cols + 20 * step_rows * width,
                "feed_forward",
            )
            full.update({0: mid, 1: h2, 2: hid, 3: gz})
            return c, part, back, cd

        fed = []
        for i in range(chunks):
            while ("out", i) not in line.results:
                line.step()
            fed.append(feed_forward(i))
            line.step(("mid", i), fed[i][2])
        mid, h2, hid, gz_gate = (full[n] for n in range(4))
        gate_c = sum(f[0] for f in fed)
        down_c = butterfly(sum(f[3] for f in fed), "head", head_size)[0] / down_coef
        for i in range(chunks):
            line.step(("down", i), fed[i][1])

        back_full = {}
        out_c = 0.0
        for i in range(chunks):
            while ("mid", i) not in line.results:
                line.step()
            dm, go, ga, c = chained(
                lambda *refs, i=i: middle_kernel(i * step_rows, *refs),
                (1,),
                [
                    smem, flat(width), at(i, width), flat(width), at(i, width), vec(width), vec(width),
                    pl.BlockSpec((1, width, attn_cols), lambda *g: (3, 0, 0)),
                ],
                [
                    lengths, line.results[("mid", i)], mid, line.results[("out", i)], cotangent,
                    feedforward_gain[None], out_coef[None], first_w,
                ],
                [
                    (shape((rows, width), F32), at(i, width)),
                    (shape((rows, width), BF), at(i, width)),
                    (shape((rows, attn_cols), BF), at(i, attn_cols)),
                    (shape((1, width), F32), vec(width)),
                ],
                dict(back_full),
                2 * step_rows * width * attn_cols,
                14 * step_rows * width,
                "middle_back",
            )
            back_full = {0: dm, 1: go, 2: ga}
            out_c = out_c + c
        grad_mid, gz_out, grad_att = (back_full[n] for n in range(3))
        out_c = out_c[0]
        gz_attn, c_attn = attend_back(lengths, qkv, grad_att, logs, attn_coef, cosine, sine, step_rows)
        for i in range(chunks):
            back = (
                mm("tc,rc->tr", gz_attn[0, spans[i]], attn_w[0])
                + mm("tc,rc->tr", gz_attn[1, spans[i]], attn_w[1])
                + mm("tc,rc->tr", gz_attn[2, spans[i]], attn_w[2])
            )
            line.step(("first", i), back.astype(BF))
        for i in range(3):
            line.step()

        output, grad_tokens = {}, {}
        for i in range(chunks):
            output = {
                0: chained(
                    lambda *refs, i=i: output_kernel(i * step_rows, *refs),
                    (1,),
                    [smem, flat(width), at(i, width), vec(width)],
                    [lengths, line.results[("down", i)], mid, down_coef[None]],
                    [(shape((rows, width), BF), at(i, width))],
                    output,
                    step_rows * width,
                    8 * step_rows * width,
                    "layer_output",
                )[0]
            }
        for i in range(chunks):
            grad_tokens = {
                0: chained(
                    tokens_kernel,
                    (1,),
                    [flat(width), at(i, width), at(i, width), vec(width)],
                    [line.results[("first", i)], tokens, grad_mid, attention_gain[None]],
                    [(shape((rows, width), F32), at(i, width))],
                    grad_tokens,
                    step_rows * width,
                    12 * step_rows * width,
                    "token_grads",
                )[0]
            }
        output, grad_tokens = output[0], grad_tokens[0]

        def column_grads(h, gz, w, inner, outer, c, n, m):
            e = -c * m / (n * n * n)
            members = gz.shape[0]
            low = jnp.concatenate([mm("tc,kc->tk", gz[p], outer[p]) for p in range(members)], 1)
            red = mm("td,dk->tk", h, inner.transpose(1, 0, 2).reshape(width, -1))
            d_inner = mm("tk,td->kd", low, h).reshape(members, rank, width)
            d_inner = SCALE * (d_inner + mm("pkc,pdc->pkd", outer * e[:, None, :], w))
            d_outer = jnp.stack(
                [mm("tk,tc->kc", red[:, p * rank : (p + 1) * rank], gz[p]) for p in range(members)]
            )
            d_outer = SCALE * (d_outer + mm("pdk,pdc->pkc", inner, w) * e[:, None, :])
            return d_inner, d_outer, c / n

        def row_grads(h, gz, w, inner, outer, c, n, m):
            e = -c * m / (n * n * n)
            low = mm("tc,kc->tk", gz, outer)
            d_inner = SCALE * (mm("tk,tr->kr", low, h) + mm("kc,cr->kr", outer * e[None, :], w))
            red = mm("tr,rk->tk", h, inner)
            d_outer = SCALE * (mm("tk,tc->kc", red, gz) + mm("rk,cr->kc", inner, w) * e[None, :])
            return d_inner, d_outer, c / n

        gz_late, h2, hid, gz_gate, gz_out, gz_down = lax.optimization_barrier(
            (gz_attn, h2, hid, gz_gate, gz_out, gz_down)
        )
        attn_di, attn_do, attn_dm = column_grads(
            h1, gz_late, attn_w, attention_inner, attention_outer, c_attn, attn_n, attention_magnitude
        )
        gate_di, gate_do, gate_dm = column_grads(
            h2, gz_gate, gate_w, gating_inner, gating_outer, gate_c, gate_n, gating_magnitude
        )
        out_di, out_do, out_dm = row_grads(
            attended, gz_out, out_w, output_inner, output_outer_factor, out_c, out_n, output_magnitude
        )
        down_di, down_do, down_dm = row_grads(
            hid, gz_down, down_w, downward_inner, down_outer_factor, down_c, down_n, downward_magnitude
        )

        def over_dp(val):
            return butterfly(val.astype(BF), "dp", dp_size)

        wide_set = [attn_di.reshape(3 * rank, width), gate_di.reshape(2 * rank, width), out_do, down_do]
        wide_set = butterfly(over_dp(jnp.concatenate(wide_set, 0)), "head", head_size)
        attn_di = wide_set[: 3 * rank].reshape(3, rank, width)
        gate_di = wide_set[3 * rank : 5 * rank].reshape(2, rank, width)
        out_do, down_do = wide_set[5 * rank : 6 * rank], wide_set[6 * rank :]
        narrow = over_dp(jnp.concatenate([attn_do.reshape(3 * rank, -1), attn_dm, out_di], 0))
        attn_do = narrow[: 3 * rank].reshape(3, rank, -1)
        attn_dm = narrow[3 * rank : 3 * rank + 3]
        out_di = narrow[3 * rank + 3 :]
        hidden = over_dp(jnp.concatenate([gate_do.reshape(2 * rank, -1), down_di, gate_dm], 0))
        gate_do = hidden[: 2 * rank].reshape(2, rank, -1)
        down_di = hidden[2 * rank : 3 * rank]
        gate_dm = hidden[3 * rank :]
        mags = over_dp(jnp.stack([out_dm, down_dm]))
        out_dm, down_dm = mags[0], mags[1]

        def wide(val):
            return val.astype(F32)

        return (
            output,
            grad_tokens,
            wide(attn_di).transpose(0, 2, 1),
            wide(attn_do),
            wide(attn_dm),
            wide(out_di).T,
            wide(out_do),
            wide(out_dm),
            wide(gate_di).transpose(0, 2, 1),
            wide(gate_do),
            wide(gate_dm),
            wide(down_di).T,
            wide(down_do),
            wide(down_dm),
        )

    return on_device


def solution(mesh):
    return jax.shard_map(
        make(mesh),
        mesh=mesh,
        in_specs=(
            P("dp", None),
            P("dp", None),
            P("dp"),
            P(),
            P(),
            P(None, "dp", "head"),
            P("head", "dp"),
            P(None, "dp", "head"),
            P("head", "dp"),
            P(),
            P(None, None, "head"),
            P(None, "head"),
            P("head", None),
            P(),
            P(),
            P(),
            P(None, None, "head"),
            P(None, "head"),
            P("head", None),
            P(),
            P(),
        ),
        out_specs=(
            P("dp", None),
            P("dp", None),
            P(),
            P(None, None, "head"),
            P(None, "head"),
            P("head", None),
            P(),
            P(),
            P(),
            P(None, None, "head"),
            P(None, "head"),
            P("head", None),
            P(),
            P(),
        ),
        check_vma=False,
    )
```

```python
import jax
import jax.numpy as jnp
from jax import lax
from jax.experimental import pallas as pl
from jax.experimental.pallas import tpu as pltpu
from jax.sharding import PartitionSpec as P

HEAD_DIM = 128
SCALE = 2.0
EPS = 1e-05
NORM_EPS = 1e-06
NEG = -1e30
BF = jnp.bfloat16
F32 = jnp.float32


def mm(spec, a, b):
    return jnp.einsum(spec, a.astype(BF), b.astype(BF), preferred_element_type=F32)


def rotary_tables(total_rows):
    position = jnp.arange(total_rows).astype(F32)[:, None]
    inverse = 10000.0 ** (-jnp.arange(0, HEAD_DIM, 2).astype(F32) / HEAD_DIM)
    angles = position * inverse[None, :]
    angles = jnp.concatenate([angles, angles], axis=1)
    return jnp.cos(angles), jnp.sin(angles)


def norm_scale(values):
    return lax.rsqrt(jnp.mean(values * values, axis=-1, keepdims=True) + EPS)


def norm_back(values, gain, grad):
    r = norm_scale(values)
    a = gain * grad
    return r * a - values * (r * r * r) * jnp.mean(values * a, axis=-1, keepdims=True)


class Line:
    def __init__(self, size):
        self.size = size
        self.mid = None
        self.out = None
        self.queue = []
        self.results = {}

    def step(self, name=None, chunk=None, beside=()):
        beside = tuple(beside)
        if self.size != 4:
            if chunk is not None:
                self.results[name] = lax.psum(chunk, "head")
            return beside
        new = None if chunk is None else (name, chunk)
        live = [v for v in (new, self.mid, self.out) if v is not None]
        held = lax.optimization_barrier(tuple(v[1] for v in live))
        held = dict(zip([v[0] for v in live], held))
        index = lax.axis_index("head")
        end = (index == 0) | (index == 3)
        sent = {}
        if new is not None:
            sent["in"] = lax.ppermute(held[new[0]], "head", [(0, 1), (3, 2)])
        if self.mid is not None:
            sent["mid"] = lax.ppermute(held[self.mid[0]], "head", [(1, 2), (2, 1)])
        if self.out is not None:
            sent["out"] = lax.ppermute(held[self.out[0]], "head", [(1, 0), (2, 3)])
        keys = list(sent)
        tied = lax.optimization_barrier(tuple(sent[k] for k in keys) + beside)
        sent = dict(zip(keys, tied))
        nxt_mid = nxt_out = None
        if self.out is not None:
            self.results[self.out[0]] = jnp.where(end, sent["out"], held[self.out[0]])
        if self.mid is not None:
            nxt_out = (self.mid[0], held[self.mid[0]] + sent["mid"])
        if new is not None:
            nxt_mid = (new[0], held[new[0]] + sent["in"])
        self.mid, self.out = nxt_mid, nxt_out
        return tied[len(keys) :]


def turn(values, cosine, sine):
    return values * cosine + pltpu.roll(values, HEAD_DIM // 2, 1) * sine


def contract(left, right, ldim, rdim):
    return lax.dot_general(
        left, right, (((ldim,), (rdim,)), ((), ())), preferred_element_type=F32
    )


def masked_scores(qc, kk, length, offset):
    scores = contract(qc, kk, 1, 1) * HEAD_DIM ** (-0.5)
    row = offset + lax.broadcasted_iota(jnp.int32, scores.shape, 0)
    col = lax.broadcasted_iota(jnp.int32, scores.shape, 1)
    return jnp.where((col <= row) & (col < length), scores, NEG)


def forward_kernel(rows, len_ref, z_ref, coef_ref, cos_ref, sin_ref, qkv_ref, out_ref, log_ref):
    total = z_ref.shape[1]
    length = len_ref[0]
    for member in range(3):
        val = z_ref[member] * coef_ref[member : member + 1, :]
        if member < 2:
            val = turn(val, cos_ref[...], sin_ref[...])
        qkv_ref[member] = val.astype(BF)
    for offset in range(0, total, rows):
        keys = offset + rows
        scores = masked_scores(qkv_ref[0, offset:keys, :], qkv_ref[1, :keys, :], length, offset)
        top = jnp.max(scores, axis=1, keepdims=True)
        shifted = jnp.exp(scores - top)
        summed = jnp.sum(shifted, axis=1, keepdims=True)
        weights = (shifted * (1.0 / summed)).astype(BF)
        out_ref[offset:keys, :] = contract(weights, qkv_ref[2, :keys, :], 1, 0).astype(BF)
        log_ref[0, offset:keys, :] = top + jnp.log(summed)


def backward_kernel(
    rows, len_ref, qkv_ref, grad_ref, log_ref, coef_ref, cos_ref, sin_ref, gz_ref, c_ref, dq, dk, dv
):
    total = qkv_ref.shape[1]
    length = len_ref[0]
    factor = HEAD_DIM ** (-0.5)
    dk[...] = jnp.zeros_like(dk)
    dv[...] = jnp.zeros_like(dv)
    for offset in range(0, total, rows):
        keys = offset + rows
        qc = qkv_ref[0, offset:keys, :]
        grad = grad_ref[offset:keys, :]
        scores = masked_scores(qc, qkv_ref[1, :keys, :], length, offset)
        weights = jnp.exp(scores - log_ref[0, offset:keys, :])
        dv[:keys, :] += contract(weights.astype(BF), grad, 0, 0)
        dw = contract(grad, qkv_ref[2, :keys, :], 1, 1)
        mean = jnp.sum(weights * dw, axis=1, keepdims=True)
        ds = (weights * (dw - mean)).astype(BF)
        dq[offset:keys, :] = contract(ds, qkv_ref[1, :keys, :], 1, 0) * factor
        dk[:keys, :] += contract(ds, qc, 0, 0)
    for member, acc in enumerate((dq, dk, dv)):
        grads = acc[...]
        unturned = qkv_ref[member].astype(F32)
        if member == 1:
            grads = grads * factor
        if member < 2:
            grads = turn(grads, cos_ref[...], -sin_ref[...])
            unturned = turn(unturned, cos_ref[...], -sin_ref[...])
        coef = coef_ref[member : member + 1, :]
        gz_ref[member] = (grads * coef).astype(BF)
        c_ref[member : member + 1, :] = jnp.sum(unturned * grads, axis=0, keepdims=True) / coef


def head_specs(total):
    three = pl.BlockSpec((3, total, HEAD_DIM), lambda h: (0, 0, h))
    flat = pl.BlockSpec((total, HEAD_DIM), lambda h: (0, h))
    small = pl.BlockSpec((3, HEAD_DIM), lambda h: (0, h))
    table = pl.BlockSpec((total, HEAD_DIM), lambda h: (0, 0))
    log = pl.BlockSpec((1, total, 1), lambda h: (h, 0, 0))
    scalar = pl.BlockSpec(memory_space=pltpu.SMEM)
    return three, flat, small, table, log, scalar


def attend(lengths, z, coef, cosine, sine, rows):
    total, cols = z.shape[1:]
    three, flat, small, table, log, scalar = head_specs(total)
    heads = cols // HEAD_DIM
    return pl.pallas_call(
        lambda *refs: forward_kernel(rows, *refs),
        grid=(heads,),
        in_specs=[scalar, three, small, table, table],
        out_specs=[three, flat, log],
        out_shape=[
            jax.ShapeDtypeStruct(z.shape, BF),
            jax.ShapeDtypeStruct((total, cols), BF),
            jax.ShapeDtypeStruct((heads, total, 1), F32),
        ],
        cost_estimate=pl.CostEstimate(
            flops=4 * total * total * cols, bytes_accessed=20 * total * cols, transcendentals=total * total * heads
        ),
        name="attend_forward",
    )(lengths, z, coef, cosine, sine)


def attend_back(lengths, qkv, grad, logs, coef, cosine, sine, rows):
    total, cols = qkv.shape[1:]
    three, flat, small, table, log, scalar = head_specs(total)
    heads = cols // HEAD_DIM
    return pl.pallas_call(
        lambda *refs: backward_kernel(rows, *refs),
        grid=(heads,),
        in_specs=[scalar, three, flat, log, small, table, table],
        out_specs=[three, small],
        out_shape=[jax.ShapeDtypeStruct(qkv.shape, BF), jax.ShapeDtypeStruct((3, cols), F32)],
        scratch_shapes=[pltpu.VMEM((total, HEAD_DIM), F32)] * 3,
        cost_estimate=pl.CostEstimate(
            flops=10 * total * total * cols, bytes_accessed=14 * total * cols, transcendentals=total * total * heads
        ),
        name="attend_backward",
    )(lengths, qkv, grad, logs, coef, cosine, sine)


def chained(kernel, grid, in_specs, args, outs, previous, flops, moved, name):
    held = [(pos, previous[pos]) for pos in sorted(previous)]
    count = len(args)

    def body(*refs):
        kernel(*refs[:count], *refs[count + len(held) :])

    return pl.pallas_call(
        body,
        grid=grid,
        in_specs=list(in_specs) + [pl.BlockSpec(memory_space=pl.ANY)] * len(held),
        out_specs=[o[1] for o in outs],
        out_shape=[o[0] for o in outs],
        input_output_aliases={count + n: pos for n, (pos, _) in enumerate(held)},
        scratch_shapes=outs_scratch(name, outs),
        cost_estimate=pl.CostEstimate(flops=flops, bytes_accessed=moved, transcendentals=0),
        name=name,
    )(*args, *[v for _, v in held])


def outs_scratch(name, outs):
    if name != "feed_forward":
        return []
    block = outs[1][1].block_shape
    return [pltpu.VMEM(block, F32), pltpu.VMEM(block, F32)]


def feed_kernel(
    x_ref, zo_ref, ocoef_ref, gain_ref, gzd_ref, w_ref, coef_ref,
    mid_ref, h2_ref, hid_ref, gz_ref, c_ref, part_ref, back_ref, cd_ref, acc_part, acc_back,
):
    step = pl.program_id(0)

    @pl.when(step == 0)
    def _():
        mid = x_ref[...].astype(F32) + zo_ref[...].astype(F32) * ocoef_ref[...]
        mid_ref[...] = mid
        h2_ref[...] = (mid * norm_scale(mid) * gain_ref[...]).astype(BF)
        acc_part[...] = jnp.zeros_like(acc_part)
        acc_back[...] = jnp.zeros_like(acc_back)

    h2 = h2_ref[...]
    zg = contract(h2, w_ref[0], 1, 0)
    zu = contract(h2, w_ref[1], 1, 0)
    dh = contract(gzd_ref[...], w_ref[2], 1, 0)
    cg, cu = coef_ref[0:1, :], coef_ref[1:2, :]
    g, u = zg * cg, zu * cu
    sg = 1.0 / (1.0 + jnp.exp(-g))
    hid = (g * sg * u).astype(BF)
    dg = dh * u * sg * (1.0 + g * (1.0 - sg))
    du = dh * g * sg
    c_ref[0:1, :] = jnp.sum(zg * dg, axis=0, keepdims=True)
    c_ref[1:2, :] = jnp.sum(zu * du, axis=0, keepdims=True)
    gg, gu = (dg * cg).astype(BF), (du * cu).astype(BF)
    gz_ref[0] = gg
    gz_ref[1] = gu
    hid_ref[...] = hid
    acc_part[...] += contract(hid, w_ref[2], 1, 1)
    both = jnp.concatenate([w_ref[0], w_ref[1]], axis=1)
    acc_back[...] += contract(jnp.concatenate([gg, gu], axis=1), both, 1, 1)

    @pl.when(step == pl.num_programs(0) - 1)
    def _():
        part = acc_part[...]
        part_ref[...] = part.astype(BF)
        back_ref[...] = acc_back[...].astype(BF)
        cd_ref[...] = jnp.sum(part * gzd_ref[...].astype(F32), axis=0, keepdims=True)


def valid_rows(length, offset, shape):
    return offset + lax.broadcasted_iota(jnp.int32, shape, 0) < length


def middle_kernel(
    offset, len_ref, z_ref, mid_ref, zo_ref, cot_ref, gain_ref, ocoef_ref, w_ref, dm_ref, go_ref, ga_ref, c_ref
):
    valid = valid_rows(len_ref[0], offset, cot_ref.shape)
    grad = jnp.where(valid, cot_ref[...].astype(F32), 0.0)
    dm = grad + norm_back(mid_ref[...], gain_ref[...], z_ref[...].astype(F32))
    dm_ref[...] = dm
    go = (dm * ocoef_ref[...]).astype(BF)
    go_ref[...] = go
    ga_ref[...] = contract(go, w_ref[0], 1, 0).astype(BF)
    c_ref[...] = jnp.sum(zo_ref[...].astype(F32) * dm, axis=0, keepdims=True)


def output_kernel(offset, len_ref, z_ref, mid_ref, coef_ref, out_ref):
    valid = valid_rows(len_ref[0], offset, mid_ref.shape)
    val = mid_ref[...] + z_ref[...].astype(F32) * coef_ref[...]
    out_ref[...] = jnp.where(valid, val, 0.0).astype(BF)


def tokens_kernel(z_ref, x_ref, dm_ref, gain_ref, out_ref):
    out_ref[...] = dm_ref[...] + norm_back(
        x_ref[...].astype(F32), gain_ref[...], z_ref[...].astype(F32)
    )


def swap(val, axis, size, hop):
    return val + lax.ppermute(val, axis, [(i, i ^ hop) for i in range(size)])


def hops_of(size):
    return [1 << n for n in range(size.bit_length() - 1)]


def butterfly(val, axis, size):
    for hop in hops_of(size):
        val = swap(val, axis, size, hop)
    return val


def make(mesh):
    head_size = mesh.shape["head"]
    dp_size = mesh.shape["dp"]

    def on_device(
        tokens,
        cotangent,
        lengths,
        attention_gain,
        feedforward_gain,
        attention_base,
        output_base,
        gating_base,
        downward_base,
        attention_inner,
        attention_outer,
        attention_magnitude,
        output_inner,
        output_outer_factor,
        output_magnitude,
        gating_inner,
        gating_outer,
        gating_magnitude,
        downward_inner,
        down_outer_factor,
        downward_magnitude,
    ):
        rows, width = tokens.shape
        length = lengths[0]
        dp = lax.axis_index("dp")
        in_rows = attention_base.shape[1]
        out_cols = output_base.shape[1]
        attn_cols = attention_base.shape[2]
        gate_cols = gating_base.shape[2]
        heads = attn_cols // HEAD_DIM
        step_rows = min(256, rows)
        chunks = rows // step_rows

        def merge_column(base, inner, outer):
            part = lax.dynamic_slice_in_dim(inner, dp * in_rows, in_rows, axis=1)
            low = mm("prk,pkc->prc", part, outer)
            return base.astype(F32) + SCALE * low

        def merge_row(base, inner, outer):
            part = lax.dynamic_slice_in_dim(outer, dp * out_cols, out_cols, axis=1)
            return base.astype(F32) + SCALE * mm("rk,kc->rc", inner, part)

        attn_part = merge_column(attention_base, attention_inner, attention_outer).astype(BF)
        out_wide = merge_row(output_base, output_inner, output_outer_factor)
        first_part = jnp.concatenate([attn_part, out_wide.astype(BF).T[None]], 0)
        first_w = lax.all_gather(first_part, "dp", axis=1, tiled=True)
        attn_w, out_w = first_w[:3], first_w[3]
        down_wide = merge_row(downward_base, downward_inner, down_outer_factor)
        gate_part = merge_column(gating_base, gating_inner, gating_outer).astype(BF)
        second_part = jnp.concatenate([gate_part, down_wide.astype(BF).T[None]], 0)
        first_w, second_part = lax.optimization_barrier((first_w, second_part))
        attn_w, out_w = first_w[:3], first_w[3]
        second_w = lax.all_gather(second_part, "dp", axis=1, tiled=True)
        gate_w, down_w = second_w[:2], second_w[2]
        row_squares = jnp.stack(
            [jnp.sum(out_wide * out_wide, axis=0), jnp.sum(down_wide * down_wide, axis=0)]
        )
        slots = (jnp.arange(dp_size) == dp).astype(F32)[None, :, None] * row_squares[:, None, :]
        slots = butterfly(butterfly(slots, "head", head_size), "dp", dp_size)
        row_squares = slots.reshape(2, width)

        x = tokens.astype(F32)
        h1 = (x * norm_scale(x) * attention_gain).astype(BF)
        cosine, sine = rotary_tables(rows)
        sine = jnp.where(jnp.arange(HEAD_DIM) < HEAD_DIM // 2, -sine, sine)
        first_w, row_squares, h1, cosine, sine = lax.optimization_barrier(
            (first_w, row_squares, h1, cosine, sine)
        )
        attn_w, out_w = first_w[:3], first_w[3]

        def squares_of(w):
            wide = w.astype(F32)
            return jnp.sum(wide * wide, axis=1)

        attn_n = jnp.sqrt(squares_of(attn_w) + NORM_EPS)
        attn_coef = attention_magnitude / attn_n
        z_attn = mm("tr,prc->ptc", h1, attn_w)
        qkv, attended, logs = attend(lengths, z_attn, attn_coef, cosine, sine, step_rows)

        row_n = jnp.sqrt(row_squares + NORM_EPS)
        out_n, down_n = row_n[0], row_n[1]
        out_coef = output_magnitude / out_n
        down_coef = downward_magnitude / down_n

        line = Line(head_size)
        spans = [slice(i * step_rows, (i + 1) * step_rows) for i in range(chunks)]
        valid = (jnp.arange(rows) < length)[:, None]
        gz_down = (jnp.where(valid, cotangent.astype(F32), 0.0) * down_coef).astype(BF)

        gate_n = jnp.sqrt(squares_of(gate_w) + NORM_EPS)
        gate_coef = gating_magnitude / gate_n
        rank = gating_inner.shape[2]

        def flat(n):
            return pl.BlockSpec((step_rows, n), lambda *g: (0, 0))

        def at(i, n):
            return pl.BlockSpec((step_rows, n), lambda *g: (i, 0))

        def vec(n):
            return pl.BlockSpec((1, n), lambda *g: (0, 0))

        def shape(dims, dtype):
            return jax.ShapeDtypeStruct(dims, dtype)

        smem = pl.BlockSpec(memory_space=pltpu.SMEM)
        lanes = 128
        blocks = gate_cols // lanes
        full = {}

        def feed_forward(i):
            outs = [
                (shape((rows, width), F32), at(i, width)),
                (shape((rows, width), BF), at(i, width)),
                (shape((rows, gate_cols), BF), pl.BlockSpec((step_rows, lanes), lambda j: (i, j))),
                (shape((2, rows, gate_cols), BF), pl.BlockSpec((2, step_rows, lanes), lambda j: (0, i, j))),
                (shape((2, gate_cols), F32), pl.BlockSpec((2, lanes), lambda j: (0, j))),
                (shape((step_rows, width), BF), flat(width)),
                (shape((step_rows, width), BF), flat(width)),
                (shape((1, width), F32), vec(width)),
            ]
            mid, h2, hid, gz, c, part, back, cd = chained(
                feed_kernel,
                (blocks,),
                [
                    at(i, width), flat(width), vec(width), vec(width), at(i, width),
                    pl.BlockSpec((3, width, lanes), lambda j: (0, 0, j)),
                    pl.BlockSpec((2, lanes), lambda j: (0, j)),
                ],
                [tokens, line.results[("out", i)], out_coef[None], feedforward_gain[None], gz_down, second_w, gate_coef],
                outs,
                {n: full[n] for n in full},
                12 * step_rows * width * gate_cols,
                6 * width * gate_cols + 20 * step_rows * width,
                "feed_forward",
            )
            full.update({0: mid, 1: h2, 2: hid, 3: gz})
            return c, part, back, cd

        def column_grads(h, gz, w, inner, outer, c, n, m):
            e = -c * m / (n * n * n)
            members = gz.shape[0]
            low = jnp.concatenate([mm("tc,kc->tk", gz[p], outer[p]) for p in range(members)], 1)
            red = mm("td,dk->tk", h, inner.transpose(1, 0, 2).reshape(width, -1))
            d_inner = mm("tk,td->kd", low, h).reshape(members, rank, width)
            d_inner = SCALE * (d_inner + mm("pkc,pdc->pkd", outer * e[:, None, :], w))
            d_outer = jnp.stack(
                [mm("tk,tc->kc", red[:, p * rank : (p + 1) * rank], gz[p]) for p in range(members)]
            )
            d_outer = SCALE * (d_outer + mm("pdk,pdc->pkc", inner, w) * e[:, None, :])
            return d_inner, d_outer, c / n

        def row_grads(h, gz, w, inner, outer, c, n, m):
            e = -c * m / (n * n * n)
            low = mm("tc,kc->tk", gz, outer)
            d_inner = SCALE * (mm("tk,tr->kr", low, h) + mm("kc,cr->kr", outer * e[None, :], w))
            red = mm("tr,rk->tk", h, inner)
            d_outer = SCALE * (mm("tk,tc->kc", red, gz) + mm("rk,cr->kc", inner, w) * e[None, :])
            return d_inner, d_outer, c / n

        back_full, output, token_sums, out_cs = {}, {}, {}, []

        def middle_back(i):
            dm, go, ga, c = chained(
                lambda *refs: middle_kernel(i * step_rows, *refs),
                (1,),
                [
                    smem, flat(width), at(i, width), flat(width), at(i, width), vec(width), vec(width),
                    pl.BlockSpec((1, width, attn_cols), lambda *g: (3, 0, 0)),
                ],
                [
                    lengths, line.results[("mid", i)], full[0], line.results[("out", i)], cotangent,
                    feedforward_gain[None], out_coef[None], first_w,
                ],
                [
                    (shape((rows, width), F32), at(i, width)),
                    (shape((rows, width), BF), at(i, width)),
                    (shape((rows, attn_cols), BF), at(i, attn_cols)),
                    (shape((1, width), F32), vec(width)),
                ],
                dict(back_full),
                2 * step_rows * width * attn_cols,
                14 * step_rows * width,
                "middle_back",
            )
            back_full.update({0: dm, 1: go, 2: ga})
            out_cs.append(c[0])
            return c

        def layer_output(i):
            output[0] = chained(
                lambda *refs: output_kernel(i * step_rows, *refs),
                (1,),
                [smem, flat(width), at(i, width), vec(width)],
                [lengths, line.results[("down", i)], full[0], down_coef[None]],
                [(shape((rows, width), BF), at(i, width))],
                dict(output),
                step_rows * width,
                8 * step_rows * width,
                "layer_output",
            )[0]

        def token_grads(i):
            token_sums[0] = chained(
                tokens_kernel,
                (1,),
                [flat(width), at(i, width), at(i, width), vec(width)],
                [line.results[("first", i)], tokens, back_full[0], attention_gain[None]],
                [(shape((rows, width), F32), at(i, width))],
                dict(token_sums),
                step_rows * width,
                12 * step_rows * width,
                "token_grads",
            )[0]

        def out_sum(i):
            return mm("tr,cr->tc", attended[spans[i]], out_w).astype(BF)

        def first_sum(i):
            back = (
                mm("tc,rc->tr", gz_attn[0, spans[i]], attn_w[0])
                + mm("tc,rc->tr", gz_attn[1, spans[i]], attn_w[1])
                + mm("tc,rc->tr", gz_attn[2, spans[i]], attn_w[2])
            )
            return back.astype(BF)

        nxt = out_sum(0)
        for i in range(2):
            (nxt,) = line.step(("out", i), nxt, (out_sum(i + 1),))
        last, gate_coef, gz_down = line.step(("out", 2), nxt, (out_sum(3), gate_coef, gz_down))[:3]
        fed = []
        for i in range(chunks):
            c, part, back, cd = feed_forward(i)
            name, chunk = (("out", 3), last) if i == 0 else (("mid", i - 1), fed[i - 1][2])
            back, part = line.step(name, chunk, (back, part))
            fed.append((c, part, back, cd))
        h2, hid, gz_gate = (full[n] for n in range(1, 4))
        gate_c = sum(f[0] for f in fed)
        down_c = sum(f[3] for f in fed)
        middle_back(0)
        head_hops = hops_of(head_size)
        down_c = swap(down_c, "head", head_size, head_hops[0])
        down_c, back_full[2] = line.step(("mid", 3), fed[3][2], (down_c, back_full[2]))
        for hop in head_hops[1:]:
            down_c = swap(down_c, "head", head_size, hop)
        middle_back(1)
        gate_di, gate_do, gate_dm = column_grads(
            h2, gz_gate, gate_w, gating_inner, gating_outer, gate_c, gate_n, gating_magnitude
        )
        down_c, back_full[2], gate_di, gate_do = line.step(
            ("down", 0), fed[0][1], (down_c, back_full[2], gate_di, gate_do)
        )
        down_c = down_c[0] / down_coef
        middle_back(2)
        down_di, down_do, down_dm = row_grads(
            hid, gz_down, down_w, downward_inner, down_outer_factor, down_c, down_n, downward_magnitude
        )
        back_full[2], down_di, down_do = line.step(
            ("down", 1), fed[1][1], (back_full[2], down_di, down_do)
        )
        middle_back(3)
        out_c = sum(out_cs)
        gz_attn, c_attn = attend_back(
            lengths, qkv, back_full[2], logs, attn_coef, cosine, sine, step_rows
        )
        gz_attn, c_attn, nxt = line.step(("down", 2), fed[2][1], (gz_attn, c_attn, first_sum(0)))
        out_di, out_do, out_dm = row_grads(
            attended, back_full[1], out_w, output_inner, output_outer_factor, out_c, out_n, output_magnitude
        )
        nxt, out_di, out_do, gz_attn = line.step(
            ("first", 0), nxt, (first_sum(1), out_di, out_do, gz_attn)
        )
        attn_di, attn_do, attn_dm = column_grads(
            h1, gz_attn, attn_w, attention_inner, attention_outer, c_attn, attn_n, attention_magnitude
        )
        nxt, attn_di, attn_do, gz_attn = line.step(
            ("first", 1), nxt, (first_sum(2), attn_di, attn_do, gz_attn)
        )
        wide_set = [attn_di.reshape(3 * rank, width), gate_di.reshape(2 * rank, width), out_do, down_do]
        groups = [
            jnp.concatenate(wide_set, 0).astype(BF),
            jnp.concatenate([attn_do.reshape(3 * rank, -1), attn_dm, out_di], 0).astype(BF),
            jnp.concatenate([gate_do.reshape(2 * rank, -1), down_di, gate_dm], 0).astype(BF),
            jnp.stack([out_dm, down_dm]).astype(BF),
        ]
        dp_hops = hops_of(dp_size)
        last_sum = first_sum(3)
        groups = [swap(g, "dp", dp_size, dp_hops[0]) for g in groups]
        layer_output(0)
        last_sum, output[0], *groups = line.step(("first", 2), nxt, (last_sum, output[0], *groups))
        groups = [swap(g, "dp", dp_size, dp_hops[1]) for g in groups]
        layer_output(1)
        output[0], *groups = line.step(("first", 3), last_sum, (output[0], *groups))
        for hop in dp_hops[2:]:
            groups = [swap(g, "dp", dp_size, hop) for g in groups]
        layer_output(2)
        token_grads(0)
        output[0], token_sums[0], *groups = line.step(
            ("down", 3), fed[3][1], (output[0], token_sums[0], *groups)
        )
        wide_set, narrow, hidden, mags = groups
        wide_set = swap(wide_set, "head", head_size, head_hops[0])
        token_grads(1)
        wide_set, token_sums[0] = line.step(None, None, (wide_set, token_sums[0]))
        for hop in head_hops[1:]:
            wide_set = swap(wide_set, "head", head_size, hop)
        token_grads(2)
        token_grads(3)
        wide_set, token_sums[0] = line.step(None, None, (wide_set, token_sums[0]))
        layer_output(3)
        output, grad_tokens = output[0], token_sums[0]

        attn_di = wide_set[: 3 * rank].reshape(3, rank, width)
        gate_di = wide_set[3 * rank : 5 * rank].reshape(2, rank, width)
        out_do, down_do = wide_set[5 * rank : 6 * rank], wide_set[6 * rank :]
        attn_do = narrow[: 3 * rank].reshape(3, rank, -1)
        attn_dm = narrow[3 * rank : 3 * rank + 3]
        out_di = narrow[3 * rank + 3 :]
        gate_do = hidden[: 2 * rank].reshape(2, rank, -1)
        down_di = hidden[2 * rank : 3 * rank]
        gate_dm = hidden[3 * rank :]
        out_dm, down_dm = mags[0], mags[1]

        def wide(val):
            return val.astype(F32)

        return (
            output,
            grad_tokens,
            wide(attn_di).transpose(0, 2, 1),
            wide(attn_do),
            wide(attn_dm),
            wide(out_di).T,
            wide(out_do),
            wide(out_dm),
            wide(gate_di).transpose(0, 2, 1),
            wide(gate_do),
            wide(gate_dm),
            wide(down_di).T,
            wide(down_do),
            wide(down_dm),
        )

    return on_device


def solution(mesh):
    return jax.shard_map(
        make(mesh),
        mesh=mesh,
        in_specs=(
            P("dp", None),
            P("dp", None),
            P("dp"),
            P(),
            P(),
            P(None, "dp", "head"),
            P("head", "dp"),
            P(None, "dp", "head"),
            P("head", "dp"),
            P(),
            P(None, None, "head"),
            P(None, "head"),
            P("head", None),
            P(),
            P(),
            P(),
            P(None, None, "head"),
            P(None, "head"),
            P("head", None),
            P(),
            P(),
        ),
        out_specs=(
            P("dp", None),
            P("dp", None),
            P(),
            P(None, None, "head"),
            P(None, "head"),
            P("head", None),
            P(),
            P(),
            P(),
            P(None, None, "head"),
            P(None, "head"),
            P("head", None),
            P(),
            P(),
        ),
        check_vma=False,
    )
```
